256 devices in a mesh: rows: 16 (over z, core), samp: 16 (over y, x).
Axes of the slice: x: 4, y: 4, z: 8, core: 2. Of those that a mesh axis runs over, the one named last changes fastest.
Arguments:
- right_sides: float32 [576, 128, 2048], P('rows', None, 'samp'), may hold values from -6 to 6
- factor_blocks: float32 [576, 6, 128, 128], P('rows', None, 'samp'), may hold values from -0.21875 to 0.21875
- block_columns: int32 [576, 6], P('rows'), may hold values from 0 to 8, as said below
- pivot_rows: int32 [8], replicated, may hold values from 0 to 575, as said below
- diag_inverse: float32 [8, 128, 128], replicated
Outputs:
- solved_blocks: float32 [8, 128, 2048], P(None, None, 'samp')
- updated_sides: float32 [576, 128, 2048], P('rows', None, 'samp')
The draws below stay inside these ranges and needn't reach their ends.
Inputs may be any that keep to these rules, and one draw needn't show every extreme that they name: `block_columns`: in each block row the values below 8 are distinct; 8 marks an empty slot. `pivot_rows`: the 8 positions are distinct.
All inputs are finite; a program needn't handle non-finite values.
Results may differ from the reference program's by a relative error of at most 0.0001.
Values sent between devices are 32-bit elements; how exact they have to be, the bound alone decides.
No kernel may reach another device: no remote copies, remote signals or barrier semaphores. Data moves between devices by JAX's collectives and lax.ppermute only.
A program may use at most 128 MiB of HBM per device.

```python
import math
import jax
import jax.numpy as jnp
from jax import lax

BLOCK = 128
STEPS = 8
SLOTS = 6
BLOCK_ROWS = 576
SAMPLES = 2048


def draw_block_columns(key, part):
    key_order, key_live = jax.random.split(jax.random.fold_in(key, 11))
    scores = jax.random.randint(key_order, (BLOCK_ROWS, STEPS), 0, 2 ** 20) * STEPS + jnp.arange(STEPS, dtype=jnp.int32)[None, :]
    ordering = jnp.argsort(scores, axis=1)[:, :SLOTS].astype(jnp.int32)
    positions = jnp.arange(BLOCK_ROWS, dtype=jnp.int32)
    live_count = jnp.minimum(SLOTS, 1 + jax.random.randint(key_live, (BLOCK_ROWS,), 0, SLOTS) + positions * SLOTS // BLOCK_ROWS)
    slot_ids = jnp.arange(SLOTS, dtype=jnp.int32)
    return jnp.where(slot_ids[None, :] < live_count[:, None], ordering, STEPS).astype(jnp.int32)


def draw_pivot_rows(key, part):
    key_perm, key_place = jax.random.split(jax.random.fold_in(key, 17))
    shuffled = jax.random.permutation(key_perm, BLOCK_ROWS - 1)[:STEPS - 1].astype(jnp.int32)
    place = jax.random.randint(key_place, (), 0, STEPS).astype(jnp.int32)
    index_ids = jnp.arange(STEPS, dtype=jnp.int32)
    source = jnp.clip(index_ids - (index_ids > place).astype(jnp.int32), 0, STEPS - 2).astype(jnp.int32)
    picked = jnp.take(shuffled, source, axis=0)
    return jnp.where(index_ids == place, BLOCK_ROWS - 1, picked).astype(jnp.int32)


def draw_diag_inverse(key, part):
    key_diag, key_off = jax.random.split(jax.random.fold_in(key, 23))
    off_part = jax.random.normal(key_off, (STEPS, BLOCK, BLOCK), jnp.float32) * (0.35 / math.sqrt(BLOCK))
    diag_part = jnp.exp(jax.random.uniform(key_diag, (STEPS, BLOCK), jnp.float32, math.log(0.7), math.log(1.4)))
    identity = jnp.eye(BLOCK, dtype=jnp.float32)
    return off_part * (1.0 - identity)[None, :, :] + diag_part[:, :, None] * identity[None, :, :]


def block_scale(key, extent, shards, smallest, high):
    loudness = 1.0
    for dim, shards_of in shards:
        draws = jax.random.uniform(jax.random.fold_in(jax.random.fold_in(key, 6), dim), (shards_of,), jnp.float32, smallest / len(shards), high / len(shards))
        loudness = loudness * jnp.repeat(jnp.exp(draws), extent[dim] // shards_of).reshape((-1,) + (1,) * (len(extent) - 1 - dim))
    return loudness


def bell_draw(key, extent, scale, limit, pieces=(), kind=jnp.bfloat16):
    array = scale * jax.random.normal(key, extent, jnp.float32)
    if pieces:
        array = array * block_scale(key, extent, pieces, -0.22, 0.18)
    return jnp.clip(array, -limit, limit).astype(kind)


def setup_inputs(seed: int = 0) -> dict:
    splits = jax.random.split(jax.random.key(seed), 6)
    return {
        "right_sides": bell_draw(splits[0], (BLOCK_ROWS, BLOCK, SAMPLES), 1.0, 6.0, ((0, 16), (2, 16)), jnp.float32),
        "factor_blocks": bell_draw(splits[1], (BLOCK_ROWS, SLOTS, BLOCK, BLOCK), (BLOCK * SLOTS) ** -0.5, 0.21875, ((0, 16), (2, 16)), jnp.float32),
        "block_columns": draw_block_columns(jax.random.fold_in(splits[5], 71), 0),
        "pivot_rows": draw_pivot_rows(jax.random.fold_in(splits[5], 71), 0),
        "diag_inverse": draw_diag_inverse(jax.random.fold_in(splits[5], 71), 0),
    }


def reference(right_sides, factor_blocks, block_columns, pivot_rows, diag_inverse):
    highest = lax.Precision.HIGHEST
    targets = jnp.arange(STEPS, dtype=jnp.int32)
    row_rank = jnp.full((BLOCK_ROWS,), STEPS, dtype=jnp.int32).at[pivot_rows].set(targets)
    live_columns = jnp.where(block_columns < row_rank[:, None], block_columns, STEPS).astype(jnp.int32)
    solved = []
    for column in range(STEPS):
        pivot_at = pivot_rows[column].astype(jnp.int32)
        running = lax.dynamic_index_in_dim(right_sides, pivot_at, 0, keepdims=False)
        row_columns = lax.dynamic_index_in_dim(live_columns, pivot_at, 0, keepdims=False)
        row_blocks = lax.dynamic_index_in_dim(factor_blocks, pivot_at, 0, keepdims=False)
        for earlier in range(column):
            block_now = jnp.sum(jnp.where((row_columns == earlier)[:, None, None], row_blocks, 0.0), axis=0)
            running = running - jnp.dot(block_now, solved[earlier], precision=highest)
        solved.append(jnp.dot(diag_inverse[column], running, precision=highest))
    stacked = jnp.stack(solved)
    padded = jnp.concatenate([stacked, jnp.zeros((1, BLOCK, SAMPLES), dtype=stacked.dtype)], axis=0)

    def one_row(operands):
        side_row, columns_row, blocks_row = operands
        picked = jnp.take(padded, columns_row, axis=0)
        return side_row - jnp.einsum("sab,sbn->an", blocks_row, picked, precision=highest)

    updated = lax.map(one_row, (right_sides, live_columns, factor_blocks))
    return stacked, updated
```

```python
import jax
import jax.numpy as jnp
from jax import lax
from jax.experimental import pallas as pl
from jax.experimental.pallas import tpu as pltpu
from jax.sharding import PartitionSpec as P

BLOCK = 128
STEPS = 8
SLOTS = 6
RANKS = 16
SLICE = BLOCK // RANKS
HALF = BLOCK // 2
TRI = 32
ROWS_PER_STEP = 4


def tri(k, i):
    return k * (k - 1) // 2 + i


TRI_PIVOT = [k for k in range(STEPS) for _ in range(k)] + [STEPS - 1] * (TRI - tri(STEPS, 0))


def split(x):
    hi = x.astype(jnp.bfloat16)
    lo = (x - hi.astype(jnp.float32)).astype(jnp.bfloat16)
    return hi, lo


def dot(a, b):
    return lax.dot_general(a, b, (((1,), (0,)), ((), ())), preferred_element_type=jnp.float32)


def dot3(a, b2):
    ah, al = split(a)
    full = dot(ah, b2)
    return full[:, :BLOCK] + full[:, BLOCK:] + dot(al, b2[:, :BLOCK])


def pair(x):
    return jnp.concatenate(split(x), axis=1)


def pack_kernel(place, columns, sides, factor, out, rows_buf, tri_buf, sem_f, sem_r, sem_o):
    copies = []
    for j in range(STEPS):
        at = place[j]
        f = pltpu.make_async_copy(factor.at[at], rows_buf.at[j], sem_f.at[j])
        f.start()
        copies.append(f)
    sides_copies = []
    for j in range(STEPS):
        at = place[j]
        for h in range(2):
            r = pltpu.make_async_copy(
                sides.at[at, pl.ds(h * HALF, HALF)], out.at[2 * j + h, pl.ds(0, HALF)], sem_r.at[2 * j + h]
            )
            r.start()
            sides_copies.append(r)
    for c in copies:
        c.wait()
    for j in range(STEPS):
        at = place[j]
        for i in range(j):
            piece = jnp.zeros((SLICE, BLOCK), jnp.float32)
            for s in range(SLOTS):
                piece = jnp.where(columns[at, s] == i, rows_buf[j, s], piece)
            b = tri(j, i)
            tri_buf[b // 2, pl.ds((b % 2) * SLICE, SLICE)] = piece
    for b in range(tri(STEPS, 0), TRI):
        tri_buf[b // 2, pl.ds((b % 2) * SLICE, SLICE)] = jnp.zeros((SLICE, BLOCK), jnp.float32)
    o = pltpu.make_async_copy(tri_buf, out.at[:, pl.ds(HALF, 2 * SLICE)], sem_o)
    o.start()
    for c in sides_copies:
        c.wait()
    o.wait()


def pack(place, columns, sides, factor):
    return pl.pallas_call(
        pack_kernel,
        out_shape=jax.ShapeDtypeStruct((RANKS, HALF + 2 * SLICE, BLOCK), jnp.float32),
        in_specs=[
            pl.BlockSpec(memory_space=pltpu.SMEM),
            pl.BlockSpec(memory_space=pltpu.SMEM),
            pl.BlockSpec(memory_space=pl.ANY),
            pl.BlockSpec(memory_space=pl.ANY),
        ],
        out_specs=pl.BlockSpec(memory_space=pl.ANY),
        scratch_shapes=[
            pltpu.VMEM((STEPS, SLOTS, SLICE, BLOCK), jnp.float32),
            pltpu.VMEM((RANKS, 2 * SLICE, BLOCK), jnp.float32),
            pltpu.SemaphoreType.DMA((STEPS,)),
            pltpu.SemaphoreType.DMA((2 * STEPS,)),
            pltpu.SemaphoreType.DMA,
        ],
        name="pack",
    )(place, columns, sides, factor)


def solve_kernel(core, gathered, mine, other, inverse, solved, pairs, side):
    flag = core[0]

    def factor(k, i):
        b = tri(k, i)
        h = b // RANKS
        own = mine[:, b % RANKS].reshape(BLOCK, BLOCK)
        far = other[:, b % RANKS].reshape(BLOCK, BLOCK)
        return jnp.where(flag == h, own, far)

    for j in range(STEPS):
        side[j] = gathered[2 * j : 2 * j + 2, :HALF].reshape(BLOCK, BLOCK)
    for j in range(STEPS):
        x = dot3(inverse[j], pair(side[j]))
        solved[j] = x
        x2 = pair(x)
        pairs[j] = x2
        for k in range(j + 1, STEPS):
            side[k] = side[k] - dot3(factor(k, j), x2)
    pairs[STEPS] = jnp.zeros((BLOCK, 2 * BLOCK), jnp.bfloat16)


def solve(core, gathered, mine, other, inverse):
    vmem = pl.BlockSpec(memory_space=pltpu.VMEM)
    return pl.pallas_call(
        solve_kernel,
        out_shape=(
            jax.ShapeDtypeStruct((STEPS, BLOCK, BLOCK), jnp.float32),
            jax.ShapeDtypeStruct((STEPS + 1, BLOCK, 2 * BLOCK), jnp.bfloat16),
        ),
        in_specs=[pl.BlockSpec(memory_space=pltpu.SMEM), vmem, vmem, vmem, vmem],
        out_specs=(vmem, vmem),
        scratch_shapes=[pltpu.VMEM((STEPS, BLOCK, BLOCK), jnp.float32)],
        name="solve",
    )(core, gathered, mine, other, inverse)


def update_kernel(picks, sides, factor, pairs, out):
    step = pl.program_id(0)
    for r in range(ROWS_PER_STEP):
        row = step * ROWS_PER_STEP + r
        hi, lo, x2 = [], [], []
        for s in range(SLOTS):
            fh, fl = split(factor[:, r, s].reshape(BLOCK, BLOCK))
            hi.append(fh)
            lo.append(fl)
            x2.append(pairs[picks[row, s]])
        hi = jnp.concatenate(hi, axis=1)
        lo = jnp.concatenate(lo, axis=1)
        x2 = jnp.concatenate(x2, axis=0)
        full = dot(hi, x2)
        out[r] = sides[r] - (full[:, :BLOCK] + full[:, BLOCK:] + dot(lo, x2[:, :BLOCK]))


def update(picks, sides, factor, pairs):
    rows = sides.shape[0]
    return pl.pallas_call(
        update_kernel,
        grid=(rows // ROWS_PER_STEP,),
        out_shape=jax.ShapeDtypeStruct(sides.shape, jnp.float32),
        in_specs=[
            pl.BlockSpec(memory_space=pltpu.SMEM),
            pl.BlockSpec((ROWS_PER_STEP, BLOCK, BLOCK), lambda g: (g, 0, 0)),
            pl.BlockSpec((RANKS, ROWS_PER_STEP, SLOTS, SLICE, BLOCK), lambda g: (0, g, 0, 0, 0)),
            pl.BlockSpec((STEPS + 1, BLOCK, 2 * BLOCK), lambda g: (0, 0, 0)),
        ],
        out_specs=pl.BlockSpec((ROWS_PER_STEP, BLOCK, BLOCK), lambda g: (g, 0, 0)),
        name="update",
    )(picks, sides, factor, pairs)


def local(right_sides, factor_blocks, block_columns, pivot_rows, diag_inverse):
    row_count = right_sides.shape[0]
    rank = lax.axis_index("rows")
    everything = lax.all_gather(factor_blocks, "samp", axis=0, tiled=False)

    owner = pivot_rows // row_count
    place = pivot_rows % row_count
    ids = rank * row_count + jnp.arange(row_count, dtype=jnp.int32)
    targets = jnp.arange(STEPS, dtype=jnp.int32)
    row_rank = STEPS + jnp.sum(jnp.where(ids[:, None] == pivot_rows[None, :], targets - STEPS, 0), axis=1)
    picks = jnp.where(block_columns < row_rank[:, None], block_columns, STEPS)

    payload = pack(place, block_columns, right_sides, factor_blocks)
    pieces = lax.all_to_all(payload, "rows", 0, 0)
    tri_owner = owner[jnp.array(TRI_PIVOT, jnp.int32)]
    part = jnp.concatenate(
        [
            lax.dynamic_slice(pieces, (owner[rank // 2], 0, 0), (1, HALF, BLOCK))[0],
            lax.dynamic_slice(pieces, (tri_owner[2 * rank], HALF, 0), (1, SLICE, BLOCK))[0],
            lax.dynamic_slice(pieces, (tri_owner[2 * rank + 1], HALF + SLICE, 0), (1, SLICE, BLOCK))[0],
        ]
    )
    gathered = lax.all_gather(part, "rows", axis=0, tiled=False)
    slices = gathered[:, HALF:].reshape(TRI, SLICE, BLOCK)
    core = rank % 2
    half = lax.dynamic_slice(slices, (core * RANKS, 0, 0), (RANKS, SLICE, BLOCK))
    mine = lax.all_to_all(jnp.broadcast_to(half, (RANKS,) + half.shape), "samp", 0, 0)
    other = lax.ppermute(mine, "rows", [(i, i ^ 1) for i in range(RANKS)])
    solved, pairs = solve(core.reshape(1), gathered, mine, other, diag_inverse)
    return solved, update(picks, right_sides, everything, pairs)


def solution(mesh):
    placed = (P("rows", None, "samp"), P("rows", None, "samp", None), P("rows", None), P(), P())
    return jax.shard_map(
        local,
        mesh=mesh,
        in_specs=placed,
        out_specs=(P(None, None, "samp"), P("rows", None, "samp")),
        check_vma=False,
    )
```

```python
import jax
import jax.numpy as jnp
from jax import lax
from jax.experimental import pallas as pl
from jax.experimental.pallas import tpu as pltpu
from jax.sharding import PartitionSpec as P

BLOCK = 128
STEPS = 8
SLOTS = 6
RANKS = 16
SLICE = BLOCK // RANKS
HALF = BLOCK // 2
TRI = 32
ROWS_PER_STEP = 12


def tri(k, i):
    return k * (k - 1) // 2 + i


TRI_PIVOT = [k for k in range(STEPS) for _ in range(k)] + [STEPS - 1] * (TRI - tri(STEPS, 0))


def split(x):
    hi = x.astype(jnp.bfloat16)
    lo = (x - hi.astype(jnp.float32)).astype(jnp.bfloat16)
    return hi, lo


def dot(a, b):
    return lax.dot_general(a, b, (((1,), (0,)), ((), ())), preferred_element_type=jnp.float32)


def dot3(a, b2):
    ah, al = split(a)
    full = dot(ah, b2)
    return full[:, :BLOCK] + full[:, BLOCK:] + dot(al, b2[:, :BLOCK])


def pair(x):
    return jnp.concatenate(split(x), axis=1)


def pack_kernel(place, columns, sides, factor, out, rows_buf, sem_f, sem_r):
    factor_copies, side_copies = [], []
    for j in range(STEPS):
        copy = pltpu.make_async_copy(factor.at[place[j]], rows_buf.at[j], sem_f.at[j])
        copy.start()
        factor_copies.append(copy)
    for j in range(STEPS):
        for h in range(2):
            copy = pltpu.make_async_copy(
                sides.at[place[j], pl.ds(h * HALF, HALF)], out.at[2 * j + h, pl.ds(0, HALF)], sem_r.at[2 * j + h]
            )
            copy.start()
            side_copies.append(copy)
    for copy in factor_copies:
        copy.wait()
    for j in range(STEPS):
        at = place[j]
        for i in range(j):
            piece = jnp.zeros((SLICE, BLOCK), jnp.float32)
            for s in range(SLOTS):
                piece = jnp.where(columns[at, s] == i, rows_buf[j, s], piece)
            b = tri(j, i)
            out[b // 2, pl.ds(HALF + (b % 2) * SLICE, SLICE)] = piece
    for b in range(tri(STEPS, 0), TRI):
        out[b // 2, pl.ds(HALF + (b % 2) * SLICE, SLICE)] = jnp.zeros((SLICE, BLOCK), jnp.float32)
    for copy in side_copies:
        copy.wait()


def pack(place, columns, sides, factor):
    smem = pl.BlockSpec(memory_space=pltpu.SMEM)
    hbm = pl.BlockSpec(memory_space=pl.ANY)
    return pl.pallas_call(
        pack_kernel,
        out_shape=jax.ShapeDtypeStruct((RANKS, HALF + 2 * SLICE, BLOCK), jnp.float32),
        in_specs=[smem, smem, hbm, hbm],
        out_specs=pl.BlockSpec(memory_space=pltpu.VMEM),
        scratch_shapes=[
            pltpu.VMEM((STEPS, SLOTS, SLICE, BLOCK), jnp.float32),
            pltpu.SemaphoreType.DMA((STEPS,)),
            pltpu.SemaphoreType.DMA((2 * STEPS,)),
        ],
        name="pack",
    )(place, columns, sides, factor)


def solve_kernel(core, gathered, mine, other, inverse, solved, pairs, side):
    flag = core[0]

    def factor(k, i):
        b = tri(k, i)
        h = b // RANKS
        own = mine[:, b % RANKS].reshape(BLOCK, BLOCK)
        far = other[:, b % RANKS].reshape(BLOCK, BLOCK)
        return jnp.where(flag == h, own, far)

    for j in range(STEPS):
        side[j] = gathered[2 * j : 2 * j + 2, :HALF].reshape(BLOCK, BLOCK)
    for j in range(STEPS):
        x = dot3(inverse[j], pair(side[j]))
        solved[j] = x
        x2 = pair(x)
        pairs[j] = x2
        for k in range(j + 1, STEPS):
            side[k] = side[k] - dot3(factor(k, j), x2)
    pairs[STEPS] = jnp.zeros((BLOCK, 2 * BLOCK), jnp.bfloat16)


def solve(core, gathered, mine, other, inverse):
    vmem = pl.BlockSpec(memory_space=pltpu.VMEM)
    return pl.pallas_call(
        solve_kernel,
        out_shape=(
            jax.ShapeDtypeStruct((STEPS, BLOCK, BLOCK), jnp.float32),
            jax.ShapeDtypeStruct((STEPS + 1, BLOCK, 2 * BLOCK), jnp.bfloat16),
        ),
        in_specs=[pl.BlockSpec(memory_space=pltpu.SMEM), vmem, vmem, vmem, vmem],
        out_specs=(vmem, vmem),
        scratch_shapes=[pltpu.VMEM((STEPS, BLOCK, BLOCK), jnp.float32)],
        name="solve",
    )(core, gathered, mine, other, inverse)


def update_kernel(picks, sides, factor, pairs, out):
    step = pl.program_id(0)
    for r in range(ROWS_PER_STEP):
        row = step * ROWS_PER_STEP + r
        hi, lo, x2 = [], [], []
        for s in range(SLOTS):
            fh, fl = split(factor[:, r, s].reshape(BLOCK, BLOCK))
            hi.append(fh)
            lo.append(fl)
            x2.append(pairs[picks[row, s]])
        hi = jnp.concatenate(hi, axis=1)
        lo = jnp.concatenate(lo, axis=1)
        x2 = jnp.concatenate(x2, axis=0)
        full = dot(hi, x2)
        out[r] = sides[r] - (full[:, :BLOCK] + full[:, BLOCK:] + dot(lo, x2[:, :BLOCK]))


def update(picks, sides, factor, pairs):
    rows = sides.shape[0]
    return pl.pallas_call(
        update_kernel,
        grid=(rows // ROWS_PER_STEP,),
        out_shape=jax.ShapeDtypeStruct(sides.shape, jnp.float32),
        in_specs=[
            pl.BlockSpec(memory_space=pltpu.SMEM),
            pl.BlockSpec((ROWS_PER_STEP, BLOCK, BLOCK), lambda g: (g, 0, 0)),
            pl.BlockSpec((RANKS, ROWS_PER_STEP, SLOTS, SLICE, BLOCK), lambda g: (0, g, 0, 0, 0)),
            pl.BlockSpec((STEPS + 1, BLOCK, 2 * BLOCK), lambda g: (0, 0, 0)),
        ],
        out_specs=pl.BlockSpec((ROWS_PER_STEP, BLOCK, BLOCK), lambda g: (g, 0, 0)),
        compiler_params=pltpu.CompilerParams(vmem_limit_bytes=48 * 2**20),
        name="update",
    )(picks, sides, factor, pairs)


def local(right_sides, factor_blocks, block_columns, pivot_rows, diag_inverse):
    row_count = right_sides.shape[0]
    rank = lax.axis_index("rows")
    everything = lax.all_gather(factor_blocks, "samp", axis=0, tiled=False)

    owner = pivot_rows // row_count
    place = pivot_rows % row_count
    ids = rank * row_count + jnp.arange(row_count, dtype=jnp.int32)
    targets = jnp.arange(STEPS, dtype=jnp.int32)
    row_rank = STEPS + jnp.sum(jnp.where(ids[:, None] == pivot_rows[None, :], targets - STEPS, 0), axis=1)
    picks = jnp.where(block_columns < row_rank[:, None], block_columns, STEPS)

    payload = pack(place, block_columns, right_sides, factor_blocks)
    pieces = lax.all_to_all(payload, "rows", 0, 0)
    tri_owner = owner[jnp.array(TRI_PIVOT, jnp.int32)]
    part = jnp.concatenate(
        [
            lax.dynamic_slice(pieces, (owner[rank // 2], 0, 0), (1, HALF, BLOCK))[0],
            lax.dynamic_slice(pieces, (tri_owner[2 * rank], HALF, 0), (1, SLICE, BLOCK))[0],
            lax.dynamic_slice(pieces, (tri_owner[2 * rank + 1], HALF + SLICE, 0), (1, SLICE, BLOCK))[0],
        ]
    )
    gathered = lax.all_gather(part, "rows", axis=0, tiled=False)
    slices = gathered[:, HALF:].reshape(TRI, SLICE, BLOCK)
    core = rank % 2
    half = lax.dynamic_slice(slices, (core * RANKS, 0, 0), (RANKS, SLICE, BLOCK))
    mine = lax.all_to_all(jnp.broadcast_to(half, (RANKS,) + half.shape), "samp", 0, 0)
    other = lax.ppermute(mine, "rows", [(i, i ^ 1) for i in range(RANKS)])
    solved, pairs = solve(core.reshape(1), gathered, mine, other, diag_inverse)
    return solved, update(picks, right_sides, everything, pairs)


def solution(mesh):
    placed = (P("rows", None, "samp"), P("rows", None, "samp", None), P("rows", None), P(), P())
    return jax.shard_map(
        local,
        mesh=mesh,
        in_specs=placed,
        out_specs=(P(None, None, "samp"), P("rows", None, "samp")),
        check_vma=False,
    )
```

```python
import jax
import jax.numpy as jnp
from jax import lax
from jax.experimental import pallas as pl
from jax.experimental.pallas import tpu as pltpu
from jax.sharding import PartitionSpec as P

BLOCK = 128
STEPS = 8
SLOTS = 6
RANKS = 16
SIDE = 4
SLICE = BLOCK // RANKS
HALF = BLOCK // 2
TRI = 32
SETS = 3
GROUP = 8
EPILOGUE_ROWS = 6


def tri(k, i):
    return k * (k - 1) // 2 + i


TRI_PIVOT = [k for k in range(STEPS) for _ in range(k)] + [STEPS - 1] * (TRI - tri(STEPS, 0))
COLUMNS_OF_Y = [[SIDE * y + x for y in range(SIDE)] for x in range(SIDE)]
ROWS_OF_X = [[SIDE * y + x for x in range(SIDE)] for y in range(SIDE)]
NEAR_X = [(i, i ^ 1) for i in range(RANKS)]
NEAR_Y = [(i, i ^ SIDE) for i in range(RANKS)]
FAR_X = [(i, i // SIDE * SIDE + SIDE - 1 - i % SIDE) for i in range(RANKS)]
FAR_Y = [(i, (SIDE - 1 - i // SIDE) * SIDE + i % SIDE) for i in range(RANKS)]
OTHER_CORE = [(i, i ^ 1) for i in range(RANKS)]


def split(x):
    hi = x.astype(jnp.bfloat16)
    lo = (x - hi.astype(jnp.float32)).astype(jnp.bfloat16)
    return hi, lo


def dot(a, b):
    return lax.dot_general(a, b, (((1,), (0,)), ((), ())), preferred_element_type=jnp.float32)


def pack_kernel(place, columns, sides, factor, out, rows_buf, sem_f, sem_r):
    factor_copies, side_copies = [], []
    for j in range(STEPS):
        copy = pltpu.make_async_copy(factor.at[place[j]], rows_buf.at[j], sem_f.at[j])
        copy.start()
        factor_copies.append(copy)
    for j in range(STEPS):
        for h in range(2):
            copy = pltpu.make_async_copy(
                sides.at[place[j], pl.ds(h * HALF, HALF)], out.at[2 * j + h, pl.ds(0, HALF)], sem_r.at[2 * j + h]
            )
            copy.start()
            side_copies.append(copy)
    for copy in factor_copies:
        copy.wait()
    for j in range(STEPS):
        at = place[j]
        for i in range(j):
            piece = jnp.zeros((SLICE, BLOCK), jnp.float32)
            for s in range(SLOTS):
                piece = jnp.where(columns[at, s] == i, rows_buf[j, s], piece)
            b = tri(j, i)
            out[b // 2, pl.ds(HALF + (b % 2) * SLICE, SLICE)] = piece
    for b in range(tri(STEPS, 0), TRI):
        out[b // 2, pl.ds(HALF + (b % 2) * SLICE, SLICE)] = jnp.zeros((SLICE, BLOCK), jnp.float32)
    for copy in side_copies:
        copy.wait()


def pack(place, columns, sides, factor):
    smem = pl.BlockSpec(memory_space=pltpu.SMEM)
    hbm = pl.BlockSpec(memory_space=pl.ANY)
    return pl.pallas_call(
        pack_kernel,
        out_shape=jax.ShapeDtypeStruct((RANKS, HALF + 2 * SLICE, BLOCK), jnp.float32),
        in_specs=[smem, smem, hbm, hbm],
        out_specs=pl.BlockSpec(memory_space=pltpu.VMEM),
        scratch_shapes=[
            pltpu.VMEM((STEPS, SLOTS, SLICE, BLOCK), jnp.float32),
            pltpu.SemaphoreType.DMA((STEPS,)),
            pltpu.SemaphoreType.DMA((2 * STEPS,)),
        ],
        name="pack",
    )(place, columns, sides, factor)


def solve_kernel(core, first, second, third, mine, other, inverse, solved, pairs, side):
    flag = core[0]

    def factor(k, i):
        b = tri(k, i)
        own = mine[:, b % RANKS].reshape(BLOCK, BLOCK)
        far = other[:, b % RANKS].reshape(BLOCK, BLOCK)
        return jnp.where(flag == b // RANKS, own, far)

    def product(a, hi, lo):
        ah, al = split(a)
        full = dot(ah, jnp.concatenate([hi, lo], axis=1))
        return full[:, : SETS * BLOCK] + full[:, SETS * BLOCK :] + dot(al, hi)

    for j in range(STEPS):
        for t, ref in enumerate((first, second, third)):
            side[j, :, t * BLOCK : (t + 1) * BLOCK] = ref[2 * j : 2 * j + 2, :HALF].reshape(BLOCK, BLOCK)
    for j in range(STEPS):
        hi, lo = split(side[j])
        x = product(inverse[j], hi, lo)
        solved[j] = x[:, :BLOCK]
        hi, lo = split(x)
        for t in range(SETS):
            pairs[t, j * BLOCK : (j + 1) * BLOCK, :BLOCK] = hi[:, t * BLOCK : (t + 1) * BLOCK]
            pairs[t, j * BLOCK : (j + 1) * BLOCK, BLOCK:] = lo[:, t * BLOCK : (t + 1) * BLOCK]
        for k in range(j + 1, STEPS):
            side[k] = side[k] - product(factor(k, j), hi, lo)


def solve(core, first, second, third, mine, other, inverse):
    vmem = pl.BlockSpec(memory_space=pltpu.VMEM)
    return pl.pallas_call(
        solve_kernel,
        out_shape=(
            jax.ShapeDtypeStruct((STEPS, BLOCK, BLOCK), jnp.float32),
            jax.ShapeDtypeStruct((SETS, STEPS * BLOCK, 2 * BLOCK), jnp.bfloat16),
        ),
        in_specs=[pl.BlockSpec(memory_space=pltpu.SMEM)] + [vmem] * 6,
        out_specs=(vmem, vmem),
        scratch_shapes=[pltpu.VMEM((STEPS, BLOCK, SETS * BLOCK), jnp.float32)],
        compiler_params=pltpu.CompilerParams(vmem_limit_bytes=48 * 2**20),
        name="solve",
    )(core, first, second, third, mine, other, inverse)


def product_kernel(partner, rows, slots, order, factor, pairs, near, far, buf, high, low, sems):
    copies = []
    for m in range(GROUP):
        copy = pltpu.make_async_copy(factor.at[order[m]], buf.at[m], sems.at[m])
        copy.start()
        copies.append(copy)
    for copy in copies:
        copy.wait()
    height = GROUP * SLICE

    def build(r, carry):
        at_row = pl.multiple_of(r * height, height)
        for c in range(STEPS):
            at = slots[r, c]
            block = buf[:, r, jnp.minimum(at, SLOTS - 1)].reshape(height, BLOCK)
            hi, lo = split(jnp.where(at < SLOTS, block, 0.0))
            high[pl.ds(at_row, height), c * BLOCK : (c + 1) * BLOCK] = hi
            low[pl.ds(at_row, height), c * BLOCK : (c + 1) * BLOCK] = lo
        return carry

    lax.fori_loop(0, rows, build, 0)
    own, theirs = pairs[0], pairs[partner]
    wide = jnp.concatenate([own, theirs], axis=1)
    tops = jnp.concatenate([own[:, :BLOCK], theirs[:, :BLOCK]], axis=1)
    chunk = rows * height // 3
    for g in range(3):
        full = dot(high[g * chunk : (g + 1) * chunk], wide)
        rest = dot(low[g * chunk : (g + 1) * chunk], tops)
        a = full[:, :BLOCK] + full[:, BLOCK : 2 * BLOCK] + rest[:, :BLOCK]
        b = full[:, 2 * BLOCK : 3 * BLOCK] + full[:, 3 * BLOCK :] + rest[:, BLOCK:]
        near[g * (rows // 3) : (g + 1) * (rows // 3)] = a.reshape(rows // 3, height, BLOCK)
        far[g * (rows // 3) : (g + 1) * (rows // 3)] = b.reshape(rows // 3, height, BLOCK)


def product(partner, slots, order, factor, pairs):
    rows = slots.shape[0]
    smem = pl.BlockSpec(memory_space=pltpu.SMEM)
    vmem = pl.BlockSpec(memory_space=pltpu.VMEM)
    height = GROUP * SLICE
    piece = jax.ShapeDtypeStruct((rows, height, BLOCK), jnp.float32)
    return pl.pallas_call(
        lambda *refs: product_kernel(partner, rows, *refs),
        out_shape=(piece, piece),
        in_specs=[smem, smem, pl.BlockSpec(memory_space=pl.ANY), vmem],
        out_specs=(vmem, vmem),
        scratch_shapes=[
            pltpu.VMEM((GROUP, rows, SLOTS, SLICE, BLOCK), jnp.float32),
            pltpu.VMEM((rows * height, STEPS * BLOCK), jnp.bfloat16),
            pltpu.VMEM((rows * height, STEPS * BLOCK), jnp.bfloat16),
            pltpu.SemaphoreType.DMA((GROUP,)),
        ],
        compiler_params=pltpu.CompilerParams(vmem_limit_bytes=48 * 2**20),
        name="product",
    )(slots, order, factor, pairs)


def finish_kernel(half_steps, spot, sides, near0, far0, near1, far1, out):
    step = pl.program_id(0)

    def place(near, far, parts, swap):
        height = BLOCK // (2 * parts)
        for r in range(EPILOGUE_ROWS):
            for q in range(parts):
                a, b = near[r, q * height : (q + 1) * height], far[r, q * height : (q + 1) * height]
                at = 2 * q * height
                out[r, at : at + height] = sides[r, at : at + height] - jnp.where(swap, b, a)
                at = at + height
                out[r, at : at + height] = sides[r, at : at + height] - jnp.where(swap, a, b)

    @pl.when(step < half_steps)
    def _():
        place(near0, far0, SIDE, spot[0] == 1)

    @pl.when(step >= half_steps)
    def _():
        place(near1, far1, 1, spot[1] == 1)


def finish(spot, sides, near0, far0, near1, far1):
    rows = sides.shape[0]
    half_steps = rows // 2 // EPILOGUE_ROWS
    height = GROUP * SLICE
    whole = pl.BlockSpec((EPILOGUE_ROWS, BLOCK, BLOCK), lambda g: (g, 0, 0))
    early = pl.BlockSpec((EPILOGUE_ROWS, height, BLOCK), lambda g: (jnp.minimum(g, half_steps - 1), 0, 0))
    late = pl.BlockSpec((EPILOGUE_ROWS, height, BLOCK), lambda g: (jnp.maximum(g - half_steps, 0), 0, 0))
    return pl.pallas_call(
        lambda *refs: finish_kernel(half_steps, *refs),
        grid=(rows // EPILOGUE_ROWS,),
        out_shape=jax.ShapeDtypeStruct(sides.shape, jnp.float32),
        in_specs=[pl.BlockSpec(memory_space=pltpu.SMEM), whole, early, early, late, late],
        out_specs=whole,
        name="finish",
    )(spot, sides, near0, far0, near1, far1)


def local(right_sides, factor_blocks, block_columns, pivot_rows, diag_inverse):
    row_count = right_sides.shape[0]
    half_rows = row_count // 2
    rank = lax.axis_index("rows")
    here = lax.axis_index("samp")
    y, x = here // SIDE, here % SIDE

    top, bottom = factor_blocks[:half_rows], factor_blocks[half_rows:]
    top = jnp.stack([top, lax.ppermute(top, "samp", NEAR_X)])
    bottom = jnp.stack([bottom, lax.ppermute(bottom, "samp", NEAR_Y)])
    shape = (GROUP, half_rows, SLOTS, SLICE, BLOCK)
    top = lax.all_gather(top, "samp", axis_index_groups=COLUMNS_OF_Y).reshape(shape)
    bottom = lax.all_gather(bottom, "samp", axis_index_groups=ROWS_OF_X).reshape(shape)
    group = jnp.arange(GROUP, dtype=jnp.int32)
    top_order = (group // 2) * 2 + ((group % 2) ^ (x % 2))
    bottom_order = (group % SIDE) * 2 + ((group // SIDE) ^ (y % 2))

    owner = pivot_rows // row_count
    place = pivot_rows % row_count
    ids = rank * row_count + jnp.arange(row_count, dtype=jnp.int32)
    targets = jnp.arange(STEPS, dtype=jnp.int32)
    row_rank = STEPS + jnp.sum(jnp.where(ids[:, None] == pivot_rows[None, :], targets - STEPS, 0), axis=1)
    picks = jnp.where(block_columns < row_rank[:, None], block_columns, STEPS)
    slots = jnp.min(
        jnp.where(picks[:, None, :] == targets[None, :, None], jnp.arange(SLOTS, dtype=jnp.int32), SLOTS), axis=2
    )

    payload = pack(place, block_columns, right_sides, factor_blocks)
    pieces = lax.all_to_all(payload, "rows", 0, 0)
    tri_owner = owner[jnp.array(TRI_PIVOT, jnp.int32)]
    part = jnp.concatenate(
        [
            lax.dynamic_slice(pieces, (owner[rank // 2], 0, 0), (1, HALF, BLOCK))[0],
            lax.dynamic_slice(pieces, (tri_owner[2 * rank], HALF, 0), (1, SLICE, BLOCK))[0],
            lax.dynamic_slice(pieces, (tri_owner[2 * rank + 1], HALF + SLICE, 0), (1, SLICE, BLOCK))[0],
        ]
    )
    gathered = lax.all_gather(part, "rows", axis=0, tiled=False)
    slices = gathered[:, HALF:].reshape(TRI, SLICE, BLOCK)
    core = rank % 2
    half = lax.dynamic_slice(slices, (core * RANKS, 0, 0), (RANKS, SLICE, BLOCK))
    mine = lax.all_to_all(jnp.broadcast_to(half, (RANKS,) + half.shape), "samp", 0, 0)
    other = lax.ppermute(mine, "rows", OTHER_CORE)
    own = gathered[:, :HALF]
    across_x = lax.ppermute(own, "samp", FAR_X)
    across_y = lax.ppermute(own, "samp", FAR_Y)
    solved, pairs = solve(core.reshape(1), own, across_x, across_y, mine, other, diag_inverse)
    near0, send0 = product(1, slots[:half_rows], top_order, top, pairs)
    far0 = lax.ppermute(send0, "samp", FAR_X)
    near1, send1 = product(2, slots[half_rows:], bottom_order, bottom, pairs)
    far1 = lax.ppermute(send1, "samp", FAR_Y)
    spot = jnp.stack([x // 2, y // 2])
    return solved, finish(spot, right_sides, near0, far0, near1, far1)


def solution(mesh):
    placed = (P("rows", None, "samp"), P("rows", None, "samp", None), P("rows", None), P(), P())
    return jax.shard_map(
        local,
        mesh=mesh,
        in_specs=placed,
        out_specs=(P(None, None, "samp"), P("rows", None, "samp")),
        check_vma=False,
    )
```

```python
import jax
import jax.numpy as jnp
from jax import lax
from jax.experimental import pallas as pl
from jax.experimental.pallas import tpu as pltpu
from jax.sharding import PartitionSpec as P

BLOCK = 128
STEPS = 8
SLOTS = 6
RANKS = 16
SIDE = 4
SLICE = BLOCK // RANKS
HALF = BLOCK // 2
TRI = 32
SETS = 3
GROUP = 8
EPILOGUE_ROWS = 9


def tri(k, i):
    return k * (k - 1) // 2 + i


TRI_PIVOT = [k for k in range(STEPS) for _ in range(k)] + [STEPS - 1] * (TRI - tri(STEPS, 0))
COLUMNS_OF_Y = [[SIDE * y + x for y in range(SIDE)] for x in range(SIDE)]
ROWS_OF_X = [[SIDE * y + x for x in range(SIDE)] for y in range(SIDE)]
NEAR_X = [(i, i ^ 1) for i in range(RANKS)]
NEAR_Y = [(i, i ^ SIDE) for i in range(RANKS)]
FAR_X = [(i, i // SIDE * SIDE + SIDE - 1 - i % SIDE) for i in range(RANKS)]
FAR_Y = [(i, (SIDE - 1 - i // SIDE) * SIDE + i % SIDE) for i in range(RANKS)]


def shift_y(d):
    return [(i, (i // SIDE + d) % SIDE * SIDE + i % SIDE) for i in range(RANKS)]


OTHER_CORE = [(i, i ^ 1) for i in range(RANKS)]


def split(x):
    hi = x.astype(jnp.bfloat16)
    lo = (x - hi.astype(jnp.float32)).astype(jnp.bfloat16)
    return hi, lo


def dot(a, b):
    return lax.dot_general(a, b, (((1,), (0,)), ((), ())), preferred_element_type=jnp.float32)


def pack_kernel(place, columns, sides, factor, out, rows_buf, sem_f, sem_r):
    factor_copies, side_copies = [], []
    for j in range(STEPS):
        copy = pltpu.make_async_copy(factor.at[place[j]], rows_buf.at[j], sem_f.at[j])
        copy.start()
        factor_copies.append(copy)
    for j in range(STEPS):
        for h in range(2):
            copy = pltpu.make_async_copy(
                sides.at[place[j], pl.ds(h * HALF, HALF)], out.at[2 * j + h, pl.ds(0, HALF)], sem_r.at[2 * j + h]
            )
            copy.start()
            side_copies.append(copy)
    for copy in factor_copies:
        copy.wait()
    for j in range(STEPS):
        at = place[j]
        for i in range(j):
            piece = jnp.zeros((SLICE, BLOCK), jnp.float32)
            for s in range(SLOTS):
                piece = jnp.where(columns[at, s] == i, rows_buf[j, s], piece)
            b = tri(j, i)
            out[b // 2, pl.ds(HALF + (b % 2) * SLICE, SLICE)] = piece
    for b in range(tri(STEPS, 0), TRI):
        out[b // 2, pl.ds(HALF + (b % 2) * SLICE, SLICE)] = jnp.zeros((SLICE, BLOCK), jnp.float32)
    for copy in side_copies:
        copy.wait()


def pack(place, columns, sides, factor):
    smem = pl.BlockSpec(memory_space=pltpu.SMEM)
    hbm = pl.BlockSpec(memory_space=pl.ANY)
    return pl.pallas_call(
        pack_kernel,
        out_shape=jax.ShapeDtypeStruct((RANKS, HALF + 2 * SLICE, BLOCK), jnp.float32),
        in_specs=[smem, smem, hbm, hbm],
        out_specs=pl.BlockSpec(memory_space=pltpu.VMEM),
        scratch_shapes=[
            pltpu.VMEM((STEPS, SLOTS, SLICE, BLOCK), jnp.float32),
            pltpu.SemaphoreType.DMA((STEPS,)),
            pltpu.SemaphoreType.DMA((2 * STEPS,)),
        ],
        name="pack",
    )(place, columns, sides, factor)


def solve_kernel(core, first, second, third, mine, other, inverse, solved, pairs, side):
    flag = core[0]

    def factor(k, i):
        b = tri(k, i)
        own = mine[:, b % RANKS].reshape(BLOCK, BLOCK)
        far = other[:, b % RANKS].reshape(BLOCK, BLOCK)
        return jnp.where(flag == b // RANKS, own, far)

    def product(a, hi, lo):
        ah, al = split(a)
        full = dot(ah, jnp.concatenate([hi, lo], axis=1))
        return full[:, : SETS * BLOCK] + full[:, SETS * BLOCK :] + dot(al, hi)

    for j in range(STEPS):
        for t, ref in enumerate((first, second, third)):
            side[j, :, t * BLOCK : (t + 1) * BLOCK] = ref[2 * j : 2 * j + 2, :HALF].reshape(BLOCK, BLOCK)
    for j in range(STEPS):
        hi, lo = split(side[j])
        x = product(inverse[j], hi, lo)
        solved[j] = x[:, :BLOCK]
        hi, lo = split(x)
        for t in range(SETS):
            pairs[t, j * BLOCK : (j + 1) * BLOCK, :BLOCK] = hi[:, t * BLOCK : (t + 1) * BLOCK]
            pairs[t, j * BLOCK : (j + 1) * BLOCK, BLOCK:] = lo[:, t * BLOCK : (t + 1) * BLOCK]
        for k in range(j + 1, STEPS):
            side[k] = side[k] - product(factor(k, j), hi, lo)


def solve(core, first, second, third, mine, other, inverse):
    vmem = pl.BlockSpec(memory_space=pltpu.VMEM)
    return pl.pallas_call(
        solve_kernel,
        out_shape=(
            jax.ShapeDtypeStruct((STEPS, BLOCK, BLOCK), jnp.float32),
            jax.ShapeDtypeStruct((SETS, STEPS * BLOCK, 2 * BLOCK), jnp.bfloat16),
        ),
        in_specs=[pl.BlockSpec(memory_space=pltpu.SMEM)] + [vmem] * 6,
        out_specs=(vmem, vmem),
        scratch_shapes=[pltpu.VMEM((STEPS, BLOCK, SETS * BLOCK), jnp.float32)],
        name="solve",
    )(core, first, second, third, mine, other, inverse)


def product_kernel(partner, rows, slots, order, mine, pair, pairs, near, far, buf, high, low, sems):
    copies = []
    for m in range(GROUP):
        source = (mine if m < SIDE else pair).at[m % SIDE]
        copy = pltpu.make_async_copy(source, buf.at[order[m]], sems.at[m])
        copy.start()
        copies.append(copy)
    for copy in copies:
        copy.wait()
    height = GROUP * SLICE

    def build(r, carry):
        at_row = pl.multiple_of(r * height, height)
        for c in range(STEPS):
            at = slots[r, c]
            block = buf[:, r, jnp.minimum(at, SLOTS - 1)].reshape(height, BLOCK)
            hi, lo = split(jnp.where(at < SLOTS, block, 0.0))
            high[pl.ds(at_row, height), c * BLOCK : (c + 1) * BLOCK] = hi
            low[pl.ds(at_row, height), c * BLOCK : (c + 1) * BLOCK] = lo
        return carry

    lax.fori_loop(0, rows, build, 0)
    own, theirs = pairs[0], pairs[partner]
    wide = jnp.concatenate([own, theirs], axis=1)
    tops = jnp.concatenate([own[:, :BLOCK], theirs[:, :BLOCK]], axis=1)
    chunk = rows * height // 3
    for g in range(3):
        full = dot(high[g * chunk : (g + 1) * chunk], wide)
        rest = dot(low[g * chunk : (g + 1) * chunk], tops)
        a = full[:, :BLOCK] + full[:, BLOCK : 2 * BLOCK] + rest[:, :BLOCK]
        b = full[:, 2 * BLOCK : 3 * BLOCK] + full[:, 3 * BLOCK :] + rest[:, BLOCK:]
        near[g * (rows // 3) : (g + 1) * (rows // 3)] = a.reshape(rows // 3, height, BLOCK)
        far[g * (rows // 3) : (g + 1) * (rows // 3)] = b.reshape(rows // 3, height, BLOCK)


def product(partner, slots, order, mine, pair, pairs):
    rows = slots.shape[0]
    smem = pl.BlockSpec(memory_space=pltpu.SMEM)
    vmem = pl.BlockSpec(memory_space=pltpu.VMEM)
    hbm = pl.BlockSpec(memory_space=pl.ANY)
    height = GROUP * SLICE
    piece = jax.ShapeDtypeStruct((rows, height, BLOCK), jnp.float32)
    return pl.pallas_call(
        lambda *refs: product_kernel(partner, rows, *refs),
        out_shape=(piece, piece),
        in_specs=[smem, smem, hbm, hbm, vmem],
        out_specs=(vmem, vmem),
        scratch_shapes=[
            pltpu.VMEM((GROUP, rows, SLOTS, SLICE, BLOCK), jnp.float32),
            pltpu.VMEM((rows * height, STEPS * BLOCK), jnp.bfloat16),
            pltpu.VMEM((rows * height, STEPS * BLOCK), jnp.bfloat16),
            pltpu.SemaphoreType.DMA((GROUP,)),
        ],
        compiler_params=pltpu.CompilerParams(vmem_limit_bytes=24 * 2**20),
        name="product",
    )(slots, order, mine, pair, pairs)


def finish_kernel(half_steps, spot, sides, near0, far0, near1, far1, out):
    step = pl.program_id(0)

    def place(near, far, parts, swap):
        height = BLOCK // (2 * parts)
        for r in range(EPILOGUE_ROWS):
            for q in range(parts):
                a, b = near[r, q * height : (q + 1) * height], far[r, q * height : (q + 1) * height]
                at = 2 * q * height
                out[r, at : at + height] = sides[r, at : at + height] - jnp.where(swap, b, a)
                at = at + height
                out[r, at : at + height] = sides[r, at : at + height] - jnp.where(swap, a, b)

    @pl.when(step < half_steps)
    def _():
        place(near0, far0, SIDE, spot[0] == 1)

    @pl.when(step >= half_steps)
    def _():
        place(near1, far1, 1, spot[1] == 1)


def finish(spot, sides, near0, far0, near1, far1):
    rows = sides.shape[0]
    half_steps = rows // 2 // EPILOGUE_ROWS
    height = GROUP * SLICE
    whole = pl.BlockSpec((EPILOGUE_ROWS, BLOCK, BLOCK), lambda g: (g, 0, 0))
    early = pl.BlockSpec((EPILOGUE_ROWS, height, BLOCK), lambda g: (jnp.minimum(g, half_steps - 1), 0, 0))
    late = pl.BlockSpec((EPILOGUE_ROWS, height, BLOCK), lambda g: (jnp.maximum(g - half_steps, 0), 0, 0))
    return pl.pallas_call(
        lambda *refs: finish_kernel(half_steps, *refs),
        grid=(rows // EPILOGUE_ROWS,),
        out_shape=jax.ShapeDtypeStruct(sides.shape, jnp.float32),
        in_specs=[pl.BlockSpec(memory_space=pltpu.SMEM), whole, early, early, late, late],
        out_specs=whole,
        name="finish",
    )(spot, sides, near0, far0, near1, far1)


def local(right_sides, factor_blocks, block_columns, pivot_rows, diag_inverse):
    row_count = right_sides.shape[0]
    half_rows = row_count // 2
    rank = lax.axis_index("rows")
    here = lax.axis_index("samp")
    y, x = here // SIDE, here % SIDE

    top, bottom = factor_blocks[:half_rows], factor_blocks[half_rows:]
    top_parts = [top] + [lax.ppermute(top, "samp", shift_y(d)) for d in (1, -1, 2)]
    bottom = lax.all_gather(bottom, "samp", axis_index_groups=ROWS_OF_X)
    seen_y = jnp.stack([y, (y + 3) % SIDE, (y + 1) % SIDE, (y + 2) % SIDE])
    seen_x = jnp.arange(SIDE, dtype=jnp.int32)
    top_order = jnp.concatenate([2 * seen_y + x % 2, 2 * seen_y + 1 - x % 2])
    bottom_order = jnp.concatenate([SIDE * (y % 2) + seen_x, SIDE * (1 - y % 2) + seen_x])

    owner = pivot_rows // row_count
    place = pivot_rows % row_count
    ids = rank * row_count + jnp.arange(row_count, dtype=jnp.int32)
    targets = jnp.arange(STEPS, dtype=jnp.int32)
    row_rank = STEPS + jnp.sum(jnp.where(ids[:, None] == pivot_rows[None, :], targets - STEPS, 0), axis=1)
    picks = jnp.where(block_columns < row_rank[:, None], block_columns, STEPS)
    slots = jnp.min(
        jnp.where(picks[:, None, :] == targets[None, :, None], jnp.arange(SLOTS, dtype=jnp.int32), SLOTS), axis=2
    )

    payload = pack(place, block_columns, right_sides, factor_blocks)
    pieces = lax.all_to_all(payload, "rows", 0, 0)
    tri_owner = owner[jnp.array(TRI_PIVOT, jnp.int32)]
    part = jnp.concatenate(
        [
            lax.dynamic_slice(pieces, (owner[rank // 2], 0, 0), (1, HALF, BLOCK))[0],
            lax.dynamic_slice(pieces, (tri_owner[2 * rank], HALF, 0), (1, SLICE, BLOCK))[0],
            lax.dynamic_slice(pieces, (tri_owner[2 * rank + 1], HALF + SLICE, 0), (1, SLICE, BLOCK))[0],
        ]
    )
    part, bottom, *top_parts = lax.optimization_barrier((part, bottom, *top_parts))
    top = jnp.stack(top_parts)
    top_pair = lax.ppermute(top, "samp", NEAR_X)
    bottom_pair = lax.ppermute(bottom, "samp", NEAR_Y)
    gathered = lax.all_gather(part, "rows", axis=0, tiled=False)
    slices = gathered[:, HALF:].reshape(TRI, SLICE, BLOCK)
    core = rank % 2
    half = lax.dynamic_slice(slices, (core * RANKS, 0, 0), (RANKS, SLICE, BLOCK))
    own = gathered[:, :HALF]
    across_x = lax.ppermute(own, "samp", FAR_X)
    across_y = lax.ppermute(own, "samp", FAR_Y)
    mine = lax.all_to_all(jnp.broadcast_to(half, (RANKS,) + half.shape), "samp", 0, 0)
    mine, across_x, across_y, top_pair, bottom_pair = lax.optimization_barrier(
        (mine, across_x, across_y, top_pair, bottom_pair)
    )
    other = lax.ppermute(mine, "rows", OTHER_CORE)
    solved, pairs = solve(core.reshape(1), own, across_x, across_y, mine, other, diag_inverse)
    near0, send0 = product(1, slots[:half_rows], top_order, top, top_pair, pairs)
    far0 = lax.ppermute(send0, "samp", FAR_X)
    near1, send1 = product(2, slots[half_rows:], bottom_order, bottom, bottom_pair, pairs)
    far1 = lax.ppermute(send1, "samp", FAR_Y)
    spot = jnp.stack([x // 2, y // 2])
    return solved, finish(spot, right_sides, near0, far0, near1, far1)


def solution(mesh):
    placed = (P("rows", None, "samp"), P("rows", None, "samp", None), P("rows", None), P(), P())
    return jax.shard_map(
        local,
        mesh=mesh,
        in_specs=placed,
        out_specs=(P(None, None, "samp"), P("rows", None, "samp")),
        check_vma=False,
    )
```

```python
import jax
import jax.numpy as jnp
from jax import lax
from jax.experimental import pallas as pl
from jax.experimental.pallas import tpu as pltpu
from jax.sharding import PartitionSpec as P

BLOCK = 128
STEPS = 8
SLOTS = 6
RANKS = 16
SIDE = 4
SLICE = BLOCK // RANKS
HALF = BLOCK // 2
TRI = 32
SETS = 2
GATHERED_ROWS = 28
ROWS_PER_STEP = 14
GROUP = 8
EPILOGUE_ROWS = 4


def tri(k, i):
    return k * (k - 1) // 2 + i


TRI_PIVOT = [k for k in range(STEPS) for _ in range(k)] + [STEPS - 1] * (TRI - tri(STEPS, 0))
NEAR_X = [(i, i ^ 1) for i in range(RANKS)]
FAR_X = [(i, i // SIDE * SIDE + SIDE - 1 - i % SIDE) for i in range(RANKS)]


def shift_y(d):
    return [(i, (i // SIDE + d) % SIDE * SIDE + i % SIDE) for i in range(RANKS)]


OTHER_CORE = [(i, i ^ 1) for i in range(RANKS)]


def split(x):
    hi = x.astype(jnp.bfloat16)
    lo = (x - hi.astype(jnp.float32)).astype(jnp.bfloat16)
    return hi, lo


def dot(a, b):
    return lax.dot_general(a, b, (((1,), (0,)), ((), ())), preferred_element_type=jnp.float32)


def pack_kernel(pivots, columns, sides, factor, out, rows_buf, sem_f, sem_r):
    row_count = sides.shape[0]
    place = [lax.rem(pivots[j], row_count) for j in range(STEPS)]
    factor_copies, side_copies = [], []
    for j in range(STEPS):
        copy = pltpu.make_async_copy(factor.at[place[j]], rows_buf.at[j], sem_f.at[j])
        copy.start()
        factor_copies.append(copy)
    for j in range(STEPS):
        for h in range(2):
            copy = pltpu.make_async_copy(
                sides.at[place[j], pl.ds(h * HALF, HALF)], out.at[2 * j + h, pl.ds(0, HALF)], sem_r.at[2 * j + h]
            )
            copy.start()
            side_copies.append(copy)
    for copy in factor_copies:
        copy.wait()
    for j in range(STEPS):
        at = place[j]
        for i in range(j):
            piece = jnp.zeros((SLICE, BLOCK), jnp.float32)
            for s in range(SLOTS):
                piece = jnp.where(columns[s, at] == i, rows_buf[j, s], piece)
            b = tri(j, i)
            out[b // 2, pl.ds(HALF + (b % 2) * SLICE, SLICE)] = piece
    for b in range(tri(STEPS, 0), TRI):
        out[b // 2, pl.ds(HALF + (b % 2) * SLICE, SLICE)] = jnp.zeros((SLICE, BLOCK), jnp.float32)
    for copy in side_copies:
        copy.wait()


def pack(pivots, columns, sides, factor):
    smem = pl.BlockSpec(memory_space=pltpu.SMEM)
    hbm = pl.BlockSpec(memory_space=pl.ANY)
    return pl.pallas_call(
        pack_kernel,
        out_shape=jax.ShapeDtypeStruct((RANKS, HALF + 2 * SLICE, BLOCK), jnp.float32),
        in_specs=[smem, smem, hbm, hbm],
        out_specs=pl.BlockSpec(memory_space=pltpu.VMEM),
        scratch_shapes=[
            pltpu.VMEM((STEPS, SLOTS, SLICE, BLOCK), jnp.float32),
            pltpu.SemaphoreType.DMA((STEPS,)),
            pltpu.SemaphoreType.DMA((2 * STEPS,)),
        ],
        name="pack",
    )(pivots, columns, sides, factor)


def solve_kernel(core, first, second, mine, other, inverse, solved, pairs, side):
    flag = core[0]

    def factor(k, i):
        b = tri(k, i)
        own = mine[:, b % RANKS].reshape(BLOCK, BLOCK)
        far = other[:, b % RANKS].reshape(BLOCK, BLOCK)
        return jnp.where(flag == b // RANKS, own, far)

    def product(a, hi, lo):
        ah, al = split(a)
        full = dot(ah, jnp.concatenate([hi, lo], axis=1))
        return full[:, : SETS * BLOCK] + full[:, SETS * BLOCK :] + dot(al, hi)

    for j in range(STEPS):
        for t, ref in enumerate((first, second)):
            side[j, :, t * BLOCK : (t + 1) * BLOCK] = ref[2 * j : 2 * j + 2, :HALF].reshape(BLOCK, BLOCK)
    for j in range(STEPS):
        hi, lo = split(side[j])
        x = product(inverse[j], hi, lo)
        solved[j] = x[:, :BLOCK]
        hi, lo = split(x)
        for t in range(SETS):
            pairs[t, j * BLOCK : (j + 1) * BLOCK, :BLOCK] = hi[:, t * BLOCK : (t + 1) * BLOCK]
            pairs[t, j * BLOCK : (j + 1) * BLOCK, BLOCK:] = lo[:, t * BLOCK : (t + 1) * BLOCK]
        for k in range(j + 1, STEPS):
            side[k] = side[k] - product(factor(k, j), hi, lo)
    for t in range(SETS):
        pairs[t, STEPS * BLOCK :] = jnp.zeros((BLOCK, 2 * BLOCK), jnp.bfloat16)


def solve(core, first, second, mine, other, inverse):
    vmem = pl.BlockSpec(memory_space=pltpu.VMEM)
    return pl.pallas_call(
        solve_kernel,
        out_shape=(
            jax.ShapeDtypeStruct((STEPS, BLOCK, BLOCK), jnp.float32),
            jax.ShapeDtypeStruct((SETS, (STEPS + 1) * BLOCK, 2 * BLOCK), jnp.bfloat16),
        ),
        in_specs=[pl.BlockSpec(memory_space=pltpu.SMEM)] + [vmem] * 5,
        out_specs=(vmem, vmem),
        scratch_shapes=[pltpu.VMEM((STEPS, BLOCK, SETS * BLOCK), jnp.float32)],
        name="solve",
    )(core, first, second, mine, other, inverse)


def product_kernel(rows, slots, order, mine, pair, pairs, near, far, buf, high, low, sems):
    copies = []
    for m in range(GROUP):
        source = (mine if m < SIDE else pair).at[m % SIDE]
        copy = pltpu.make_async_copy(source, buf.at[order[m]], sems.at[m])
        copy.start()
        copies.append(copy)
    for copy in copies:
        copy.wait()
    height = GROUP * SLICE

    def build(r, carry):
        at_row = pl.multiple_of(r * height, height)
        for c in range(STEPS):
            at = slots[r, c]
            block = buf[:, r, jnp.minimum(at, SLOTS - 1)].reshape(height, BLOCK)
            hi, lo = split(jnp.where(at < SLOTS, block, 0.0))
            high[pl.ds(at_row, height), c * BLOCK : (c + 1) * BLOCK] = hi
            low[pl.ds(at_row, height), c * BLOCK : (c + 1) * BLOCK] = lo
        return carry

    lax.fori_loop(0, rows, build, 0)
    own, theirs = pairs[0, : STEPS * BLOCK], pairs[1, : STEPS * BLOCK]
    wide = jnp.concatenate([own, theirs], axis=1)
    tops = jnp.concatenate([own[:, :BLOCK], theirs[:, :BLOCK]], axis=1)
    full = dot(high[...], wide)
    rest = dot(low[...], tops)
    a = full[:, :BLOCK] + full[:, BLOCK : 2 * BLOCK] + rest[:, :BLOCK]
    b = full[:, 2 * BLOCK : 3 * BLOCK] + full[:, 3 * BLOCK :] + rest[:, BLOCK:]
    near[...] = a.reshape(rows, height, BLOCK)
    far[...] = b.reshape(rows, height, BLOCK)


def product(slots, order, mine, pair, pairs):
    rows = slots.shape[0]
    smem = pl.BlockSpec(memory_space=pltpu.SMEM)
    vmem = pl.BlockSpec(memory_space=pltpu.VMEM)
    hbm = pl.BlockSpec(memory_space=pl.ANY)
    height = GROUP * SLICE
    piece = jax.ShapeDtypeStruct((rows, height, BLOCK), jnp.float32)
    return pl.pallas_call(
        lambda *refs: product_kernel(rows, *refs),
        out_shape=(piece, piece),
        in_specs=[smem, smem, hbm, hbm, vmem],
        out_specs=(vmem, vmem),
        scratch_shapes=[
            pltpu.VMEM((GROUP, rows, SLOTS, SLICE, BLOCK), jnp.float32),
            pltpu.VMEM((rows * height, STEPS * BLOCK), jnp.bfloat16),
            pltpu.VMEM((rows * height, STEPS * BLOCK), jnp.bfloat16),
            pltpu.SemaphoreType.DMA((GROUP,)),
        ],
        name="product",
    )(slots, order, mine, pair, pairs)


def update_kernel(picks, sides, factor, pairs, out):
    step = pl.program_id(0)
    for r in range(ROWS_PER_STEP):
        row = step * ROWS_PER_STEP + r
        hi, lo, x2 = [], [], []
        for s in range(SLOTS):
            fh, fl = split(factor[:, r, s].reshape(BLOCK, BLOCK))
            hi.append(fh)
            lo.append(fl)
            at = pl.multiple_of(picks[row, s] * BLOCK, BLOCK)
            x2.append(pairs[0, pl.ds(at, BLOCK)])
        hi = jnp.concatenate(hi, axis=1)
        lo = jnp.concatenate(lo, axis=1)
        x2 = jnp.concatenate(x2, axis=0)
        full = dot(hi, x2)
        out[r] = sides[r] - (full[:, :BLOCK] + full[:, BLOCK:] + dot(lo, x2[:, :BLOCK]))


def update(picks, sides, factor, pairs):
    rows = factor.shape[1]
    return pl.pallas_call(
        update_kernel,
        grid=(rows // ROWS_PER_STEP,),
        out_shape=jax.ShapeDtypeStruct(sides.shape, jnp.float32),
        in_specs=[
            pl.BlockSpec(memory_space=pltpu.SMEM),
            pl.BlockSpec((ROWS_PER_STEP, BLOCK, BLOCK), lambda g: (g, 0, 0)),
            pl.BlockSpec((RANKS, ROWS_PER_STEP, SLOTS, SLICE, BLOCK), lambda g: (0, g, 0, 0, 0)),
            pl.BlockSpec((1, (STEPS + 1) * BLOCK, 2 * BLOCK), lambda g: (0, 0, 0)),
        ],
        out_specs=pl.BlockSpec((ROWS_PER_STEP, BLOCK, BLOCK), lambda g: (g, 0, 0)),
        compiler_params=pltpu.CompilerParams(vmem_limit_bytes=48 * 2**20),
        name="update",
    )(picks, sides, factor, pairs)


def finish_kernel(spot, sides, near, far, base, out):
    swap = spot[0] == 1
    height = BLOCK // (2 * SIDE)
    for r in range(EPILOGUE_ROWS):
        for q in range(SIDE):
            a, b = near[r, q * height : (q + 1) * height], far[r, q * height : (q + 1) * height]
            at = 2 * q * height
            out[r, at : at + height] = sides[r, at : at + height] - jnp.where(swap, b, a)
            at = at + height
            out[r, at : at + height] = sides[r, at : at + height] - jnp.where(swap, a, b)


def finish(spot, sides, near, far, base):
    first = GATHERED_ROWS // EPILOGUE_ROWS
    height = GROUP * SLICE
    whole = pl.BlockSpec((EPILOGUE_ROWS, BLOCK, BLOCK), lambda g: (g + first, 0, 0))
    piece = pl.BlockSpec((EPILOGUE_ROWS, height, BLOCK), lambda g: (g, 0, 0))
    return pl.pallas_call(
        finish_kernel,
        grid=(near.shape[0] // EPILOGUE_ROWS,),
        out_shape=jax.ShapeDtypeStruct(sides.shape, jnp.float32),
        in_specs=[pl.BlockSpec(memory_space=pltpu.SMEM), whole, piece, piece, pl.BlockSpec(memory_space=pl.ANY)],
        out_specs=whole,
        input_output_aliases={4: 0},
        name="finish",
    )(spot, sides, near, far, base)


def local(right_sides, factor_blocks, block_columns, pivot_rows, diag_inverse):
    row_count = right_sides.shape[0]
    rank = lax.axis_index("rows")
    here = lax.axis_index("samp")
    y, x = here // SIDE, here % SIDE

    everything = lax.all_gather(factor_blocks[:GATHERED_ROWS], "samp", axis=0, tiled=False)
    rest = factor_blocks[GATHERED_ROWS:]
    rest_parts = [rest] + [lax.ppermute(rest, "samp", shift_y(d)) for d in (1, -1, 2)]
    seen_y = jnp.stack([y, (y + 3) % SIDE, (y + 1) % SIDE, (y + 2) % SIDE])
    order = jnp.concatenate([2 * seen_y + x % 2, 2 * seen_y + 1 - x % 2])

    owner = pivot_rows // row_count
    ids = rank * row_count + jnp.arange(row_count, dtype=jnp.int32)
    targets = jnp.arange(STEPS, dtype=jnp.int32)
    row_rank = STEPS + jnp.sum(jnp.where(ids[:, None] == pivot_rows[None, :], targets - STEPS, 0), axis=1)
    picks = jnp.where(block_columns < row_rank[:, None], block_columns, STEPS)
    slots = jnp.min(
        jnp.where(picks[:, None, :] == targets[None, :, None], jnp.arange(SLOTS, dtype=jnp.int32), SLOTS), axis=2
    )

    payload = pack(pivot_rows, block_columns.T, right_sides, factor_blocks)
    pieces = lax.all_to_all(payload, "rows", 0, 0)
    tri_owner = owner[jnp.array(TRI_PIVOT, jnp.int32)]
    part = jnp.concatenate(
        [
            lax.dynamic_slice(pieces, (owner[rank // 2], 0, 0), (1, HALF, BLOCK))[0],
            lax.dynamic_slice(pieces, (tri_owner[2 * rank], HALF, 0), (1, SLICE, BLOCK))[0],
            lax.dynamic_slice(pieces, (tri_owner[2 * rank + 1], HALF + SLICE, 0), (1, SLICE, BLOCK))[0],
        ]
    )
    part, *rest_parts = lax.optimization_barrier((part, *rest_parts))
    rest = jnp.stack(rest_parts)
    rest_pair = lax.ppermute(rest, "samp", NEAR_X)
    gathered = lax.all_gather(part, "rows", axis=0, tiled=False)
    slices = gathered[:, HALF:].reshape(TRI, SLICE, BLOCK)
    core = rank % 2
    half = lax.dynamic_slice(slices, (core * RANKS, 0, 0), (RANKS, SLICE, BLOCK))
    own = gathered[:, :HALF]
    across = lax.ppermute(own, "samp", FAR_X)
    mine = lax.all_to_all(jnp.broadcast_to(half, (RANKS,) + half.shape), "samp", 0, 0)
    mine, across, rest_pair = lax.optimization_barrier((mine, across, rest_pair))
    other = lax.ppermute(mine, "rows", OTHER_CORE)
    solved, pairs = solve(core.reshape(1), own, across, mine, other, diag_inverse)
    near, send = product(slots[GATHERED_ROWS:], order, rest, rest_pair, pairs)
    far = lax.ppermute(send, "samp", FAR_X)
    updated = update(picks, right_sides, everything, pairs)
    return solved, finish((x // 2).reshape(1), right_sides, near, far, updated)


def solution(mesh):
    placed = (P("rows", None, "samp"), P("rows", None, "samp", None), P("rows", None), P(), P())
    return jax.shard_map(
        local,
        mesh=mesh,
        in_specs=placed,
        out_specs=(P(None, None, "samp"), P("rows", None, "samp")),
        check_vma=False,
    )
```

```python
import jax
import jax.numpy as jnp
from jax import lax
from jax.experimental import pallas as pl
from jax.experimental.pallas import tpu as pltpu
from jax.sharding import PartitionSpec as P

BLOCK = 128
STEPS = 8
SLOTS = 6
RANKS = 16
SIDE = 4
SLICE = BLOCK // RANKS
HALF = BLOCK // 2
TRI = 32
MOVES = (1, -1, 2)
SETS = 1 + 2 * len(MOVES)
STRIP = SIDE * SLICE
EPILOGUE_ROWS = 9


def tri(k, i):
    return k * (k - 1) // 2 + i


def shift_y(d):
    return [(i, (i // SIDE + d) % SIDE * SIDE + i % SIDE) for i in range(RANKS)]


def shift_x(d):
    return [(i, i // SIDE * SIDE + (i % SIDE + d) % SIDE) for i in range(RANKS)]


TRI_PIVOT = [k for k in range(STEPS) for _ in range(k)] + [STEPS - 1] * (TRI - tri(STEPS, 0))
COLUMNS_OF_Y = [[SIDE * y + x for y in range(SIDE)] for x in range(SIDE)]
ROWS_OF_X = [[SIDE * y + x for x in range(SIDE)] for y in range(SIDE)]
OTHER_CORE = [(i, i ^ 1) for i in range(RANKS)]


def split(x):
    hi = x.astype(jnp.bfloat16)
    lo = (x - hi.astype(jnp.float32)).astype(jnp.bfloat16)
    return hi, lo


def dot(a, b):
    return lax.dot_general(a, b, (((1,), (0,)), ((), ())), preferred_element_type=jnp.float32)


def pack_kernel(pivots, columns, sides, factor, out, rows_buf, sem_f, sem_r):
    row_count = sides.shape[0]
    place = [lax.rem(pivots[j], row_count) for j in range(STEPS)]
    factor_copies, side_copies = [], []
    for j in range(STEPS):
        copy = pltpu.make_async_copy(factor.at[place[j]], rows_buf.at[j], sem_f.at[j])
        copy.start()
        factor_copies.append(copy)
    for j in range(STEPS):
        for h in range(2):
            copy = pltpu.make_async_copy(
                sides.at[place[j], pl.ds(h * HALF, HALF)], out.at[2 * j + h, pl.ds(0, HALF)], sem_r.at[2 * j + h]
            )
            copy.start()
            side_copies.append(copy)
    for copy in factor_copies:
        copy.wait()
    for j in range(STEPS):
        at = place[j]
        for i in range(j):
            piece = jnp.zeros((SLICE, BLOCK), jnp.float32)
            for s in range(SLOTS):
                piece = jnp.where(columns[s, at] == i, rows_buf[j, s], piece)
            b = tri(j, i)
            out[b // 2, pl.ds(HALF + (b % 2) * SLICE, SLICE)] = piece
    for b in range(tri(STEPS, 0), TRI):
        out[b // 2, pl.ds(HALF + (b % 2) * SLICE, SLICE)] = jnp.zeros((SLICE, BLOCK), jnp.float32)
    for copy in side_copies:
        copy.wait()


def pack(pivots, columns, sides, factor):
    smem = pl.BlockSpec(memory_space=pltpu.SMEM)
    hbm = pl.BlockSpec(memory_space=pl.ANY)
    return pl.pallas_call(
        pack_kernel,
        out_shape=jax.ShapeDtypeStruct((RANKS, HALF + 2 * SLICE, BLOCK), jnp.float32),
        in_specs=[smem, smem, hbm, hbm],
        out_specs=pl.BlockSpec(memory_space=pltpu.VMEM),
        scratch_shapes=[
            pltpu.VMEM((STEPS, SLOTS, SLICE, BLOCK), jnp.float32),
            pltpu.SemaphoreType.DMA((STEPS,)),
            pltpu.SemaphoreType.DMA((2 * STEPS,)),
        ],
        name="pack",
    )(pivots, columns, sides, factor)


def solve_kernel(core, own, sides_here, sides_there, mine, other, inverse, solved, pairs, side):
    flag = core[0]

    def factor(k, i):
        b = tri(k, i)
        near = mine[:, b % RANKS].reshape(BLOCK, BLOCK)
        far = other[:, b % RANKS].reshape(BLOCK, BLOCK)
        return jnp.where(flag == b // RANKS, near, far)

    def product(a, hi, lo):
        ah, al = split(a)
        return dot(ah, hi) + dot(ah, lo) + dot(al, hi)

    quarter = STEPS // 2
    for j in range(STEPS):
        side[j, :, :BLOCK] = own[2 * j : 2 * j + 2, :HALF].reshape(BLOCK, BLOCK)
        at = 2 * (j % quarter)
        for t in range(1, SETS):
            near = sides_here[t - 1, at : at + 2].reshape(BLOCK, BLOCK)
            far = sides_there[t - 1, at : at + 2].reshape(BLOCK, BLOCK)
            side[j, :, t * BLOCK : (t + 1) * BLOCK] = jnp.where(flag == j // quarter, near, far)
    for j in range(STEPS):
        hi, lo = split(side[j])
        x = product(inverse[j], hi, lo)
        solved[j] = x[:, :BLOCK]
        hi, lo = split(x)
        for t in range(SETS):
            pairs[t, j * BLOCK : (j + 1) * BLOCK, :BLOCK] = hi[:, t * BLOCK : (t + 1) * BLOCK]
            pairs[t, j * BLOCK : (j + 1) * BLOCK, BLOCK:] = lo[:, t * BLOCK : (t + 1) * BLOCK]
        for k in range(j + 1, STEPS):
            side[k] = side[k] - product(factor(k, j), hi, lo)


def solve(core, own, sides_here, sides_there, mine, other, inverse):
    vmem = pl.BlockSpec(memory_space=pltpu.VMEM)
    return pl.pallas_call(
        solve_kernel,
        out_shape=(
            jax.ShapeDtypeStruct((STEPS, BLOCK, BLOCK), jnp.float32),
            jax.ShapeDtypeStruct((SETS, STEPS * BLOCK, 2 * BLOCK), jnp.bfloat16),
        ),
        in_specs=[pl.BlockSpec(memory_space=pltpu.SMEM)] + [vmem] * 6,
        out_specs=(vmem, vmem),
        scratch_shapes=[pltpu.VMEM((STEPS, BLOCK, SETS * BLOCK), jnp.float32)],
        compiler_params=pltpu.CompilerParams(vmem_limit_bytes=28 * 2**20),
        name="solve",
    )(core, own, sides_here, sides_there, mine, other, inverse)


def product_kernel(first_set, rows, slots, factor, pairs, *rest):
    outs, (high, low) = rest[: 1 + len(MOVES)], rest[1 + len(MOVES) :]

    def build(r, carry):
        at_row = pl.multiple_of(r * STRIP, STRIP)
        for c in range(STEPS):
            at = slots[r, c]
            block = factor[:, r, jnp.minimum(at, SLOTS - 1)].reshape(STRIP, BLOCK)
            hi, lo = split(jnp.where(at < SLOTS, block, 0.0))
            high[pl.ds(at_row, STRIP), c * BLOCK : (c + 1) * BLOCK] = hi
            low[pl.ds(at_row, STRIP), c * BLOCK : (c + 1) * BLOCK] = lo
        return carry

    lax.fori_loop(0, rows, build, 0)
    sets = (0,) + tuple(range(first_set, first_set + len(MOVES)))
    for t, out in zip(sets, outs):
        full = dot(high[...], pairs[t])
        small = dot(low[...], pairs[t, :, :BLOCK])
        out[...] = (full[:, :BLOCK] + full[:, BLOCK:] + small).reshape(rows, STRIP, BLOCK)


def product(first_set, slots, factor, pairs):
    rows = slots.shape[0]
    vmem = pl.BlockSpec(memory_space=pltpu.VMEM)
    piece = jax.ShapeDtypeStruct((rows, STRIP, BLOCK), jnp.float32)
    return pl.pallas_call(
        lambda *refs: product_kernel(first_set, rows, *refs),
        out_shape=(piece,) * (1 + len(MOVES)),
        in_specs=[pl.BlockSpec(memory_space=pltpu.SMEM), vmem, vmem],
        out_specs=(vmem,) * (1 + len(MOVES)),
        scratch_shapes=[pltpu.VMEM((rows * STRIP, STEPS * BLOCK), jnp.bfloat16)] * 2,
        compiler_params=pltpu.CompilerParams(vmem_limit_bytes=24 * 2**20),
        name="product",
    )(slots, factor, pairs)


def finish_kernel(half_steps, spots, sides, *refs):
    step = pl.program_id(0)
    out = refs[-1]
    count = 1 + len(MOVES)
    tops, bottoms = refs[:count], refs[count : 2 * count]

    @pl.when(step < half_steps)
    def _():
        for t, ref in enumerate(tops):
            for r in range(EPILOGUE_ROWS):
                for q in range(SIDE):
                    at = pl.multiple_of(STRIP * q + SLICE * spots[0, t], SLICE)
                    out[r, pl.ds(at, SLICE)] = sides[r, pl.ds(at, SLICE)] - ref[r, SLICE * q : SLICE * (q + 1)]

    @pl.when(step >= half_steps)
    def _():
        for t, ref in enumerate(bottoms):
            at = pl.multiple_of(STRIP * spots[1, t], STRIP)
            out[:, pl.ds(at, STRIP)] = sides[:, pl.ds(at, STRIP)] - ref[...]


def finish(spots, sides, tops, bottoms):
    rows = sides.shape[0]
    half_steps = rows // 2 // EPILOGUE_ROWS
    whole = pl.BlockSpec((EPILOGUE_ROWS, BLOCK, BLOCK), lambda g: (g, 0, 0))
    early = pl.BlockSpec((EPILOGUE_ROWS, STRIP, BLOCK), lambda g: (jnp.minimum(g, half_steps - 1), 0, 0))
    late = pl.BlockSpec((EPILOGUE_ROWS, STRIP, BLOCK), lambda g: (jnp.maximum(g - half_steps, 0), 0, 0))
    return pl.pallas_call(
        lambda *refs: finish_kernel(half_steps, *refs),
        grid=(rows // EPILOGUE_ROWS,),
        out_shape=jax.ShapeDtypeStruct(sides.shape, jnp.float32),
        in_specs=[pl.BlockSpec(memory_space=pltpu.SMEM), whole] + [early] * len(tops) + [late] * len(bottoms),
        out_specs=whole,
        name="finish",
    )(spots, sides, *tops, *bottoms)


def local(right_sides, factor_blocks, block_columns, pivot_rows, diag_inverse):
    row_count = right_sides.shape[0]
    half_rows = row_count // 2
    rank = lax.axis_index("rows")
    here = lax.axis_index("samp")
    y, x = here // SIDE, here % SIDE

    top = lax.all_gather(factor_blocks[:half_rows], "samp", axis_index_groups=COLUMNS_OF_Y)
    bottom = lax.all_gather(factor_blocks[half_rows:], "samp", axis_index_groups=ROWS_OF_X)

    owner = pivot_rows // row_count
    ids = rank * row_count + jnp.arange(row_count, dtype=jnp.int32)
    targets = jnp.arange(STEPS, dtype=jnp.int32)
    row_rank = STEPS + jnp.sum(jnp.where(ids[:, None] == pivot_rows[None, :], targets - STEPS, 0), axis=1)
    picks = jnp.where(block_columns < row_rank[:, None], block_columns, STEPS)
    slots = jnp.min(
        jnp.where(picks[:, None, :] == targets[None, :, None], jnp.arange(SLOTS, dtype=jnp.int32), SLOTS), axis=2
    )

    payload = pack(pivot_rows, block_columns.T, right_sides, factor_blocks)
    pieces = lax.all_to_all(payload, "rows", 0, 0)
    tri_owner = owner[jnp.array(TRI_PIVOT, jnp.int32)]
    part = jnp.concatenate(
        [
            lax.dynamic_slice(pieces, (owner[rank // 2], 0, 0), (1, HALF, BLOCK))[0],
            lax.dynamic_slice(pieces, (tri_owner[2 * rank], HALF, 0), (1, SLICE, BLOCK))[0],
            lax.dynamic_slice(pieces, (tri_owner[2 * rank + 1], HALF + SLICE, 0), (1, SLICE, BLOCK))[0],
        ]
    )
    gathered = lax.all_gather(part, "rows", axis=0, tiled=False)
    gathered, top = lax.optimization_barrier((gathered, top))
    core = rank % 2
    slices = gathered[:, HALF:].reshape(TRI, SLICE, BLOCK)
    half = lax.dynamic_slice(slices, (core * RANKS, 0, 0), (RANKS, SLICE, BLOCK))
    own = gathered[:, :HALF]
    share = lax.dynamic_slice(own, (core * STEPS, 0, 0), (STEPS, HALF, BLOCK))
    shares = [lax.ppermute(share, "samp", shift(-d)) for shift in (shift_x, shift_y) for d in MOVES]
    mine = lax.all_to_all(jnp.broadcast_to(half, (RANKS,) + half.shape), "samp", 0, 0)
    mine, bottom, *shares = lax.optimization_barrier((mine, bottom, *shares))
    sides_here = jnp.stack(shares)
    sides_there = lax.ppermute(sides_here, "rows", OTHER_CORE)
    other = lax.ppermute(mine, "rows", OTHER_CORE)
    solved, pairs = solve(core.reshape(1), own, sides_here, sides_there, mine, other, diag_inverse)
    tops = list(product(1, slots[:half_rows], top, pairs))
    tops[1:] = [lax.ppermute(v, "samp", shift_x(d)) for v, d in zip(tops[1:], MOVES)]
    bottoms = list(product(1 + len(MOVES), slots[half_rows:], bottom, pairs))
    bottoms[1:] = [lax.ppermute(v, "samp", shift_y(d)) for v, d in zip(bottoms[1:], MOVES)]
    steps = jnp.array((0,) + MOVES, jnp.int32)
    spots = (jnp.stack([x, y])[:, None] - steps[None, :] + SIDE) % SIDE
    return solved, finish(spots, right_sides, tops, bottoms)


def solution(mesh):
    placed = (P("rows", None, "samp"), P("rows", None, "samp", None), P("rows", None), P(), P())
    return jax.shard_map(
        local,
        mesh=mesh,
        in_specs=placed,
        out_specs=(P(None, None, "samp"), P("rows", None, "samp")),
        check_vma=False,
    )
```

```python
import jax
import jax.numpy as jnp
from jax import lax
from jax.experimental import pallas as pl
from jax.experimental.pallas import tpu as pltpu
from jax.sharding import PartitionSpec as P

BLOCK = 128
STEPS = 8
SLOTS = 6
RANKS = 16
SLICE = BLOCK // RANKS
HALF = BLOCK // 2
TRI = 32
ROWS_PER_STEP = 18
SIDE = 4
MOVES = (1, -1, 2)
PART = 8


def shift_y(d):
    return [(i, (i // SIDE + d) % SIDE * SIDE + i % SIDE) for i in range(RANKS)]


def shift_x(d):
    return [(i, i // SIDE * SIDE + (i % SIDE + d) % SIDE) for i in range(RANKS)]


def tri(k, i):
    return k * (k - 1) // 2 + i


TRI_PIVOT = [k for k in range(STEPS) for _ in range(k)] + [STEPS - 1] * (TRI - tri(STEPS, 0))


def split(x):
    hi = x.astype(jnp.bfloat16)
    lo = (x - hi.astype(jnp.float32)).astype(jnp.bfloat16)
    return hi, lo


def dot(a, b):
    return lax.dot_general(a, b, (((1,), (0,)), ((), ())), preferred_element_type=jnp.float32)


def dot3(a, b2):
    ah, al = split(a)
    full = dot(ah, b2)
    return full[:, :BLOCK] + full[:, BLOCK:] + dot(al, b2[:, :BLOCK])


def pair(x):
    return jnp.concatenate(split(x), axis=1)


def pack_kernel(pivots, columns, sides, factor, out, rows_buf, sem_f, sem_r):
    row_count = sides.shape[0]
    place = [lax.rem(pivots[j], row_count) for j in range(STEPS)]
    factor_copies, side_copies = [], []
    for j in range(STEPS):
        copy = pltpu.make_async_copy(factor.at[place[j]], rows_buf.at[j], sem_f.at[j])
        copy.start()
        factor_copies.append(copy)
    for j in range(STEPS):
        for h in range(2):
            copy = pltpu.make_async_copy(
                sides.at[place[j], pl.ds(h * HALF, HALF)], out.at[2 * j + h, pl.ds(0, HALF)], sem_r.at[2 * j + h]
            )
            copy.start()
            side_copies.append(copy)
    for copy in factor_copies:
        copy.wait()
    for j in range(STEPS):
        at = place[j]
        for i in range(j):
            piece = jnp.zeros((SLICE, BLOCK), jnp.float32)
            for s in range(SLOTS):
                piece = jnp.where(columns[s, at] == i, rows_buf[j, s], piece)
            b = tri(j, i)
            out[b // 2, pl.ds(HALF + (b % 2) * SLICE, SLICE)] = piece
    for b in range(tri(STEPS, 0), TRI):
        out[b // 2, pl.ds(HALF + (b % 2) * SLICE, SLICE)] = jnp.zeros((SLICE, BLOCK), jnp.float32)
    for copy in side_copies:
        copy.wait()


def pack(pivots, columns, sides, factor):
    smem = pl.BlockSpec(memory_space=pltpu.SMEM)
    hbm = pl.BlockSpec(memory_space=pl.ANY)
    return pl.pallas_call(
        pack_kernel,
        out_shape=jax.ShapeDtypeStruct((RANKS, HALF + 2 * SLICE, BLOCK), jnp.float32),
        in_specs=[smem, smem, hbm, hbm],
        out_specs=pl.BlockSpec(memory_space=pltpu.VMEM),
        scratch_shapes=[
            pltpu.VMEM((STEPS, SLOTS, SLICE, BLOCK), jnp.float32),
            pltpu.SemaphoreType.DMA((STEPS,)),
            pltpu.SemaphoreType.DMA((2 * STEPS,)),
        ],
        name="pack",
    )(pivots, columns, sides, factor)


def solve_kernel(core, spots, gathered, mine, other, inverse, solved, pairs, side, blocks):
    flag = core[0]
    for pieces, base in ((mine, 2 * PART * flag), (other, 2 * PART * (1 - flag))):
        for p in range(2):
            for e in range(SIDE):
                for d in range(SIDE):
                    at = pl.multiple_of(SLICE * spots[p, SIDE * e + d], SLICE)
                    for i in range(PART):
                        blocks[base + PART * p + i, pl.ds(at, SLICE)] = pieces[p, e, d, i]

    def factor(k, i):
        return blocks[tri(k, i)]

    for j in range(STEPS):
        side[j] = gathered[2 * j : 2 * j + 2, :HALF].reshape(BLOCK, BLOCK)
    for j in range(STEPS):
        x = dot3(inverse[j], pair(side[j]))
        solved[j] = x
        x2 = pair(x)
        pairs[j] = x2
        for k in range(j + 1, STEPS):
            side[k] = side[k] - dot3(factor(k, j), x2)
    pairs[STEPS] = jnp.zeros((BLOCK, 2 * BLOCK), jnp.bfloat16)


def solve(core, spots, gathered, mine, other, inverse):
    vmem = pl.BlockSpec(memory_space=pltpu.VMEM)
    return pl.pallas_call(
        solve_kernel,
        out_shape=(
            jax.ShapeDtypeStruct((STEPS, BLOCK, BLOCK), jnp.float32),
            jax.ShapeDtypeStruct((STEPS + 1, BLOCK, 2 * BLOCK), jnp.bfloat16),
        ),
        in_specs=[pl.BlockSpec(memory_space=pltpu.SMEM)] * 2 + [vmem] * 4,
        out_specs=(vmem, vmem),
        scratch_shapes=[
            pltpu.VMEM((STEPS, BLOCK, BLOCK), jnp.float32),
            pltpu.VMEM((TRI, BLOCK, BLOCK), jnp.float32),
        ],
        name="solve",
    )(core, spots, gathered, mine, other, inverse)


def update_kernel(picks, sides, factor, pairs, out):
    step = pl.program_id(0)
    for r in range(ROWS_PER_STEP):
        row = step * ROWS_PER_STEP + r
        hi, lo, x2 = [], [], []
        for s in range(SLOTS):
            fh, fl = split(factor[:, r, s].reshape(BLOCK, BLOCK))
            hi.append(fh)
            lo.append(fl)
            x2.append(pairs[picks[row, s]])
        hi = jnp.concatenate(hi, axis=1)
        lo = jnp.concatenate(lo, axis=1)
        x2 = jnp.concatenate(x2, axis=0)
        full = dot(hi, x2)
        out[r] = sides[r] - (full[:, :BLOCK] + full[:, BLOCK:] + dot(lo, x2[:, :BLOCK]))


def update(picks, sides, factor, pairs):
    rows = sides.shape[0]
    return pl.pallas_call(
        update_kernel,
        grid=(rows // ROWS_PER_STEP,),
        out_shape=jax.ShapeDtypeStruct(sides.shape, jnp.float32),
        in_specs=[
            pl.BlockSpec(memory_space=pltpu.SMEM),
            pl.BlockSpec((ROWS_PER_STEP, BLOCK, BLOCK), lambda g: (g, 0, 0)),
            pl.BlockSpec((RANKS, ROWS_PER_STEP, SLOTS, SLICE, BLOCK), lambda g: (0, g, 0, 0, 0)),
            pl.BlockSpec((STEPS + 1, BLOCK, 2 * BLOCK), lambda g: (0, 0, 0)),
        ],
        out_specs=pl.BlockSpec((ROWS_PER_STEP, BLOCK, BLOCK), lambda g: (g, 0, 0)),
        compiler_params=pltpu.CompilerParams(vmem_limit_bytes=48 * 2**20),
        name="update",
    )(picks, sides, factor, pairs)


def local(right_sides, factor_blocks, block_columns, pivot_rows, diag_inverse):
    row_count = right_sides.shape[0]
    rank = lax.axis_index("rows")
    everything = lax.all_gather(factor_blocks, "samp", axis=0, tiled=False)

    owner = pivot_rows // row_count
    ids = rank * row_count + jnp.arange(row_count, dtype=jnp.int32)
    targets = jnp.arange(STEPS, dtype=jnp.int32)
    row_rank = STEPS + jnp.sum(jnp.where(ids[:, None] == pivot_rows[None, :], targets - STEPS, 0), axis=1)
    picks = jnp.where(block_columns < row_rank[:, None], block_columns, STEPS)

    payload = pack(pivot_rows, block_columns.T, right_sides, factor_blocks)
    pieces = lax.all_to_all(payload, "rows", 0, 0)
    tri_owner = owner[jnp.array(TRI_PIVOT, jnp.int32)]
    part = jnp.concatenate(
        [
            lax.dynamic_slice(pieces, (owner[rank // 2], 0, 0), (1, HALF, BLOCK))[0],
            lax.dynamic_slice(pieces, (tri_owner[2 * rank], HALF, 0), (1, SLICE, BLOCK))[0],
            lax.dynamic_slice(pieces, (tri_owner[2 * rank + 1], HALF + SLICE, 0), (1, SLICE, BLOCK))[0],
        ]
    )
    gathered = lax.all_gather(part, "rows", axis=0, tiled=False)
    slices = gathered[:, HALF:].reshape(TRI, SLICE, BLOCK)
    core = rank % 2
    half = lax.dynamic_slice(slices, (core * RANKS, 0, 0), (RANKS, SLICE, BLOCK))
    first, second = half[:PART], half[PART:]
    first = [first] + [lax.ppermute(first, "samp", shift_y(d)) for d in MOVES]
    second = [second] + [lax.ppermute(second, "samp", shift_x(d)) for d in MOVES]
    first, second = jnp.stack(first), jnp.stack(second)
    parts = [first] + [lax.ppermute(first, "samp", shift_x(d)) for d in MOVES]
    parts += [second] + [lax.ppermute(second, "samp", shift_y(d)) for d in MOVES]
    mine = jnp.stack(parts).reshape(2, SIDE, SIDE, PART, SLICE, BLOCK)
    other = lax.ppermute(mine, "rows", [(i, i ^ 1) for i in range(RANKS)])
    here = lax.axis_index("samp")
    moves = jnp.array((0,) + MOVES, jnp.int32)
    y, x = (here // SIDE - moves + SIDE) % SIDE, (here % SIDE - moves + SIDE) % SIDE
    spots = jnp.stack([SIDE * y[None, :] + x[:, None], SIDE * y[:, None] + x[None, :]]).reshape(2, RANKS)
    solved, pairs = solve(core.reshape(1), spots, gathered, mine, other, diag_inverse)
    return solved, update(picks, right_sides, everything, pairs)


def solution(mesh):
    placed = (P("rows", None, "samp"), P("rows", None, "samp", None), P("rows", None), P(), P())
    return jax.shard_map(
        local,
        mesh=mesh,
        in_specs=placed,
        out_specs=(P(None, None, "samp"), P("rows", None, "samp")),
        check_vma=False,
    )
```

```python
import jax
import jax.numpy as jnp
from jax import lax
from jax.experimental import pallas as pl
from jax.experimental.pallas import tpu as pltpu
from jax.sharding import PartitionSpec as P

BLOCK = 128
STEPS = 8
SLOTS = 6
RANKS = 16
SLICE = BLOCK // RANKS
HALF = BLOCK // 2
TRI = 32
CHUNK = 6
SIDE = 4
MOVES = (1, -1, 2)
PART = 7


def shift_y(d):
    return [(i, (i // SIDE + d) % SIDE * SIDE + i % SIDE) for i in range(RANKS)]


def shift_x(d):
    return [(i, i // SIDE * SIDE + (i % SIDE + d) % SIDE) for i in range(RANKS)]


def tri(k, i):
    return k * (k - 1) // 2 + i


TRI_PIVOT = [k for k in range(STEPS) for _ in range(k)] + [STEPS - 1] * (TRI - tri(STEPS, 0))


def split(x):
    hi = x.astype(jnp.bfloat16)
    lo = (x - hi.astype(jnp.float32)).astype(jnp.bfloat16)
    return hi, lo


def dot(a, b):
    return lax.dot_general(a, b, (((1,), (0,)), ((), ())), preferred_element_type=jnp.float32)


def dot3(a, b2):
    ah, al = split(a)
    full = dot(ah, b2)
    return full[:, :BLOCK] + full[:, BLOCK:] + dot(al, b2[:, :BLOCK])


def pair(x):
    return jnp.concatenate(split(x), axis=1)


def pack_kernel(pivots, columns, sides, factor, out, rows_buf, sem_f, sem_r):
    row_count = sides.shape[0]
    place = [lax.rem(pivots[j], row_count) for j in range(STEPS)]
    factor_copies, side_copies = [], []
    for j in range(STEPS):
        copy = pltpu.make_async_copy(factor.at[place[j]], rows_buf.at[j], sem_f.at[j])
        copy.start()
        factor_copies.append(copy)
    for j in range(STEPS):
        for h in range(2):
            copy = pltpu.make_async_copy(
                sides.at[place[j], pl.ds(h * HALF, HALF)], out.at[2 * j + h, pl.ds(0, HALF)], sem_r.at[2 * j + h]
            )
            copy.start()
            side_copies.append(copy)
    for copy in factor_copies:
        copy.wait()
    for j in range(STEPS):
        at = place[j]
        for i in range(j):
            piece = jnp.zeros((SLICE, BLOCK), jnp.float32)
            for s in range(SLOTS):
                piece = jnp.where(columns[s, at] == i, rows_buf[j, s], piece)
            b = tri(j, i)
            out[b // 2, pl.ds(HALF + (b % 2) * SLICE, SLICE)] = piece
    for b in range(tri(STEPS, 0), TRI):
        out[b // 2, pl.ds(HALF + (b % 2) * SLICE, SLICE)] = jnp.zeros((SLICE, BLOCK), jnp.float32)
    for copy in side_copies:
        copy.wait()


def pack(pivots, columns, sides, factor):
    smem = pl.BlockSpec(memory_space=pltpu.SMEM)
    hbm = pl.BlockSpec(memory_space=pl.ANY)
    return pl.pallas_call(
        pack_kernel,
        out_shape=jax.ShapeDtypeStruct((RANKS, HALF + 2 * SLICE, BLOCK), jnp.float32),
        in_specs=[smem, smem, hbm, hbm],
        out_specs=pl.BlockSpec(memory_space=pltpu.VMEM),
        scratch_shapes=[
            pltpu.VMEM((STEPS, SLOTS, SLICE, BLOCK), jnp.float32),
            pltpu.SemaphoreType.DMA((STEPS,)),
            pltpu.SemaphoreType.DMA((2 * STEPS,)),
        ],
        name="pack",
    )(pivots, columns, sides, factor)


def solve_kernel(core, spots, gathered, mine, other, inverse, solved, pairs, side, blocks):
    flag = core[0]
    for pieces, base in ((mine, 2 * PART * flag), (other, 2 * PART * (1 - flag))):
        for p in range(2):
            for e in range(SIDE):
                for d in range(SIDE):
                    at = pl.multiple_of(SLICE * spots[p, SIDE * e + d], SLICE)
                    for i in range(PART):
                        blocks[base + PART * p + i, pl.ds(at, SLICE)] = pieces[p, e, d, i]

    def factor(k, i):
        return blocks[tri(k, i)]

    for j in range(STEPS):
        side[j] = gathered[2 * j : 2 * j + 2, :HALF].reshape(BLOCK, BLOCK)
    for j in range(STEPS):
        x = dot3(inverse[j], pair(side[j]))
        solved[j] = x
        x2 = pair(x)
        pairs[j] = x2
        for k in range(j + 1, STEPS):
            side[k] = side[k] - dot3(factor(k, j), x2)
    pairs[STEPS] = jnp.zeros((BLOCK, 2 * BLOCK), jnp.bfloat16)


def solve(core, spots, gathered, mine, other, inverse):
    vmem = pl.BlockSpec(memory_space=pltpu.VMEM)
    return pl.pallas_call(
        solve_kernel,
        out_shape=(
            jax.ShapeDtypeStruct((STEPS, BLOCK, BLOCK), jnp.float32),
            jax.ShapeDtypeStruct((STEPS + 1, BLOCK, 2 * BLOCK), jnp.bfloat16),
        ),
        in_specs=[pl.BlockSpec(memory_space=pltpu.SMEM)] * 2 + [vmem] * 4,
        out_specs=(vmem, vmem),
        scratch_shapes=[
            pltpu.VMEM((STEPS, BLOCK, BLOCK), jnp.float32),
            pltpu.VMEM((TRI, BLOCK, BLOCK), jnp.float32),
        ],
        name="solve",
    )(core, spots, gathered, mine, other, inverse)


def update_kernel(picks, sides, factor, pairs, out, blocks, work, solved, sem_factor, sem_side, sem_pairs, sem_out):
    count = sides.shape[0] // CHUNK

    def fetch(g):
        rows = pl.ds(g * CHUNK, CHUNK)
        return pltpu.make_async_copy(factor.at[:, rows], blocks.at[:, rows], sem_factor.at[g])

    def store(g):
        rows = pl.ds(g * CHUNK, CHUNK)
        return pltpu.make_async_copy(work.at[rows], out.at[rows], sem_out.at[g])

    side_copy = pltpu.make_async_copy(sides, work, sem_side)
    pairs_copy = pltpu.make_async_copy(pairs, solved, sem_pairs)
    pairs_copy.start()
    fetch(0).start()
    side_copy.start()
    for g in range(1, count):
        fetch(g).start()
    pairs_copy.wait()
    side_copy.wait()

    def step(g, carry):
        fetch(g).wait()
        for i in range(CHUNK):
            row = g * CHUNK + i
            hi, lo, x2 = [], [], []
            for s in range(SLOTS):
                fh, fl = split(blocks[:, row, s].reshape(BLOCK, BLOCK))
                hi.append(fh)
                lo.append(fl)
                x2.append(solved[picks[row, s]])
            hi = jnp.concatenate(hi, axis=1)
            lo = jnp.concatenate(lo, axis=1)
            x2 = jnp.concatenate(x2, axis=0)
            full = dot(hi, x2)
            work[row] = work[row] - (full[:, :BLOCK] + full[:, BLOCK:] + dot(lo, x2[:, :BLOCK]))
        store(g).start()
        return carry

    lax.fori_loop(0, count, step, 0)
    for g in range(count):
        store(g).wait()


def update(picks, sides, factor, pairs):
    hbm = pl.BlockSpec(memory_space=pl.ANY)
    count = sides.shape[0] // CHUNK
    return pl.pallas_call(
        update_kernel,
        out_shape=jax.ShapeDtypeStruct(sides.shape, jnp.float32),
        in_specs=[pl.BlockSpec(memory_space=pltpu.SMEM), hbm, hbm, hbm],
        out_specs=hbm,
        scratch_shapes=[
            pltpu.VMEM(factor.shape, jnp.float32),
            pltpu.VMEM(sides.shape, jnp.float32),
            pltpu.VMEM(pairs.shape, jnp.bfloat16),
            pltpu.SemaphoreType.DMA((count,)),
            pltpu.SemaphoreType.DMA,
            pltpu.SemaphoreType.DMA,
            pltpu.SemaphoreType.DMA((count,)),
        ],
        compiler_params=pltpu.CompilerParams(vmem_limit_bytes=58 * 2**20),
        name="update",
    )(picks, sides, factor, pairs)


def local(right_sides, factor_blocks, block_columns, pivot_rows, diag_inverse):
    row_count = right_sides.shape[0]
    rank = lax.axis_index("rows")
    everything = lax.all_gather(factor_blocks, "samp", axis=0, tiled=False)

    owner = pivot_rows // row_count
    ids = rank * row_count + jnp.arange(row_count, dtype=jnp.int32)
    targets = jnp.arange(STEPS, dtype=jnp.int32)
    row_rank = STEPS + jnp.sum(jnp.where(ids[:, None] == pivot_rows[None, :], targets - STEPS, 0), axis=1)
    picks = jnp.where(block_columns < row_rank[:, None], block_columns, STEPS)

    payload = pack(pivot_rows, block_columns.T, right_sides, factor_blocks)
    pieces = lax.all_to_all(payload, "rows", 0, 0)
    tri_owner = owner[jnp.array(TRI_PIVOT, jnp.int32)]
    part = jnp.concatenate(
        [
            lax.dynamic_slice(pieces, (owner[rank // 2], 0, 0), (1, HALF, BLOCK))[0],
            lax.dynamic_slice(pieces, (tri_owner[2 * rank], HALF, 0), (1, SLICE, BLOCK))[0],
            lax.dynamic_slice(pieces, (tri_owner[2 * rank + 1], HALF + SLICE, 0), (1, SLICE, BLOCK))[0],
        ]
    )
    gathered = lax.all_gather(part, "rows", axis=0, tiled=False)
    slices = gathered[:, HALF:].reshape(TRI, SLICE, BLOCK)
    core = rank % 2
    half = lax.dynamic_slice(slices, (core * 2 * PART, 0, 0), (2 * PART, SLICE, BLOCK))
    first, second = half[:PART], half[PART:]
    first = [first] + [lax.ppermute(first, "samp", shift_y(d)) for d in MOVES]
    second = [second] + [lax.ppermute(second, "samp", shift_x(d)) for d in MOVES]
    first, second = jnp.stack(first), jnp.stack(second)
    parts = [first] + [lax.ppermute(first, "samp", shift_x(d)) for d in MOVES]
    parts += [second] + [lax.ppermute(second, "samp", shift_y(d)) for d in MOVES]
    mine = jnp.stack(parts).reshape(2, SIDE, SIDE, PART, SLICE, BLOCK)
    other = lax.ppermute(mine, "rows", [(i, i ^ 1) for i in range(RANKS)])
    here = lax.axis_index("samp")
    moves = jnp.array((0,) + MOVES, jnp.int32)
    y, x = (here // SIDE - moves + SIDE) % SIDE, (here % SIDE - moves + SIDE) % SIDE
    spots = jnp.stack([SIDE * y[None, :] + x[:, None], SIDE * y[:, None] + x[None, :]]).reshape(2, RANKS)
    solved, pairs = solve(core.reshape(1), spots, gathered, mine, other, diag_inverse)
    return solved, update(picks, right_sides, everything, pairs)


def solution(mesh):
    placed = (P("rows", None, "samp"), P("rows", None, "samp", None), P("rows", None), P(), P())
    return jax.shard_map(
        local,
        mesh=mesh,
        in_specs=placed,
        out_specs=(P(None, None, "samp"), P("rows", None, "samp")),
        check_vma=False,
    )
```

```python
import jax
import jax.numpy as jnp
from jax import lax
from jax.experimental import pallas as pl
from jax.experimental.pallas import tpu as pltpu
from jax.sharding import PartitionSpec as P

BLOCK = 128
STEPS = 8
SLOTS = 6
RANKS = 16
SLICE = BLOCK // RANKS
HALF = BLOCK // 2
TRI = 32
ROWS_PER_STEP = 18
SIDE = 4
MOVES = (1, -1, 2)
PART = 7


def shift_y(d):
    return [(i, (i // SIDE + d) % SIDE * SIDE + i % SIDE) for i in range(RANKS)]


def shift_x(d):
    return [(i, i // SIDE * SIDE + (i % SIDE + d) % SIDE) for i in range(RANKS)]


def tri(k, i):
    return k * (k - 1) // 2 + i


TRI_PIVOT = [k for k in range(STEPS) for _ in range(k)] + [STEPS - 1] * (TRI - tri(STEPS, 0))


def split(x):
    hi = x.astype(jnp.bfloat16)
    lo = (x - hi.astype(jnp.float32)).astype(jnp.bfloat16)
    return hi, lo


def dot(a, b):
    return lax.dot_general(a, b, (((1,), (0,)), ((), ())), preferred_element_type=jnp.float32)


def dot3(a, b2):
    ah, al = split(a)
    full = dot(ah, b2)
    return full[:, :BLOCK] + full[:, BLOCK:] + dot(al, b2[:, :BLOCK])


def pair(x):
    return jnp.concatenate(split(x), axis=1)


def pack_kernel(pivots, columns, sides, factor, out, rows_buf, sem_f, sem_r):
    row_count = sides.shape[0]
    place = [lax.rem(pivots[j], row_count) for j in range(STEPS)]
    factor_copies, side_copies = [], []
    for j in range(STEPS):
        copy = pltpu.make_async_copy(factor.at[place[j]], rows_buf.at[j], sem_f.at[j])
        copy.start()
        factor_copies.append(copy)
    for j in range(STEPS):
        for h in range(2):
            copy = pltpu.make_async_copy(
                sides.at[place[j], pl.ds(h * HALF, HALF)], out.at[2 * j + h, pl.ds(0, HALF)], sem_r.at[2 * j + h]
            )
            copy.start()
            side_copies.append(copy)
    for copy in factor_copies:
        copy.wait()
    for j in range(STEPS):
        at = place[j]
        for i in range(j):
            piece = jnp.zeros((SLICE, BLOCK), jnp.float32)
            for s in range(SLOTS):
                piece = jnp.where(columns[s, at] == i, rows_buf[j, s], piece)
            b = tri(j, i)
            out[b // 2, pl.ds(HALF + (b % 2) * SLICE, SLICE)] = piece
    for b in range(tri(STEPS, 0), TRI):
        out[b // 2, pl.ds(HALF + (b % 2) * SLICE, SLICE)] = jnp.zeros((SLICE, BLOCK), jnp.float32)
    for copy in side_copies:
        copy.wait()


def pack(pivots, columns, sides, factor):
    smem = pl.BlockSpec(memory_space=pltpu.SMEM)
    hbm = pl.BlockSpec(memory_space=pl.ANY)
    return pl.pallas_call(
        pack_kernel,
        out_shape=jax.ShapeDtypeStruct((RANKS, HALF + 2 * SLICE, BLOCK), jnp.float32),
        in_specs=[smem, smem, hbm, hbm],
        out_specs=pl.BlockSpec(memory_space=pltpu.VMEM),
        scratch_shapes=[
            pltpu.VMEM((STEPS, SLOTS, SLICE, BLOCK), jnp.float32),
            pltpu.SemaphoreType.DMA((STEPS,)),
            pltpu.SemaphoreType.DMA((2 * STEPS,)),
        ],
        name="pack",
    )(pivots, columns, sides, factor)


def solve_kernel(core, spots, gathered, mine, other, inverse, solved, pairs, side, blocks):
    flag = core[0]
    for pieces, base in ((mine, 2 * PART * flag), (other, 2 * PART * (1 - flag))):
        for p in range(2):
            for e in range(SIDE):
                for d in range(SIDE):
                    at = pl.multiple_of(SLICE * spots[p, SIDE * e + d], SLICE)
                    for i in range(PART):
                        blocks[base + PART * p + i, pl.ds(at, SLICE)] = pieces[p, e, d, i]

    def factor(k, i):
        return blocks[tri(k, i)]

    for j in range(STEPS):
        side[j] = gathered[2 * j : 2 * j + 2, :HALF].reshape(BLOCK, BLOCK)
    for j in range(STEPS):
        x = dot3(inverse[j], pair(side[j]))
        solved[j] = x
        x2 = pair(x)
        pairs[j] = x2
        for k in range(j + 1, STEPS):
            side[k] = side[k] - dot3(factor(k, j), x2)
    pairs[STEPS] = jnp.zeros((BLOCK, 2 * BLOCK), jnp.bfloat16)


def solve(core, spots, gathered, mine, other, inverse):
    vmem = pl.BlockSpec(memory_space=pltpu.VMEM)
    return pl.pallas_call(
        solve_kernel,
        out_shape=(
            jax.ShapeDtypeStruct((STEPS, BLOCK, BLOCK), jnp.float32),
            jax.ShapeDtypeStruct((STEPS + 1, BLOCK, 2 * BLOCK), jnp.bfloat16),
        ),
        in_specs=[pl.BlockSpec(memory_space=pltpu.SMEM)] * 2 + [vmem] * 4,
        out_specs=(vmem, vmem),
        scratch_shapes=[
            pltpu.VMEM((STEPS, BLOCK, BLOCK), jnp.float32),
            pltpu.VMEM((TRI, BLOCK, BLOCK), jnp.float32),
        ],
        name="solve",
    )(core, spots, gathered, mine, other, inverse)


def update_kernel(picks, sides, factor, pairs, out):
    step = pl.program_id(0)
    for r in range(ROWS_PER_STEP):
        row = step * ROWS_PER_STEP + r
        hi, lo, x2 = [], [], []
        for s in range(SLOTS):
            fh, fl = split(factor[:, r, s].reshape(BLOCK, BLOCK))
            hi.append(fh)
            lo.append(fl)
            x2.append(pairs[picks[row, s]])
        hi = jnp.concatenate(hi, axis=1)
        lo = jnp.concatenate(lo, axis=1)
        x2 = jnp.concatenate(x2, axis=0)
        full = dot(hi, x2)
        out[r] = sides[r] - (full[:, :BLOCK] + full[:, BLOCK:] + dot(lo, x2[:, :BLOCK]))


def update(picks, sides, factor, pairs):
    rows = sides.shape[0]
    return pl.pallas_call(
        update_kernel,
        grid=(rows // ROWS_PER_STEP,),
        out_shape=jax.ShapeDtypeStruct(sides.shape, jnp.float32),
        in_specs=[
            pl.BlockSpec(memory_space=pltpu.SMEM),
            pl.BlockSpec((ROWS_PER_STEP, BLOCK, BLOCK), lambda g: (g, 0, 0)),
            pl.BlockSpec((RANKS, ROWS_PER_STEP, SLOTS, SLICE, BLOCK), lambda g: (0, g, 0, 0, 0)),
            pl.BlockSpec((STEPS + 1, BLOCK, 2 * BLOCK), lambda g: (0, 0, 0)),
        ],
        out_specs=pl.BlockSpec((ROWS_PER_STEP, BLOCK, BLOCK), lambda g: (g, 0, 0)),
        compiler_params=pltpu.CompilerParams(vmem_limit_bytes=58 * 2**20),
        name="update",
    )(picks, sides, factor, pairs)


def local(right_sides, factor_blocks, block_columns, pivot_rows, diag_inverse):
    row_count = right_sides.shape[0]
    rank = lax.axis_index("rows")
    everything = lax.all_gather(factor_blocks, "samp", axis=0, tiled=False)

    owner = pivot_rows // row_count
    ids = rank * row_count + jnp.arange(row_count, dtype=jnp.int32)
    targets = jnp.arange(STEPS, dtype=jnp.int32)
    row_rank = STEPS + jnp.sum(jnp.where(ids[:, None] == pivot_rows[None, :], targets - STEPS, 0), axis=1)
    picks = jnp.where(block_columns < row_rank[:, None], block_columns, STEPS)

    payload = pack(pivot_rows, block_columns.T, right_sides, factor_blocks)
    pieces = lax.all_to_all(payload, "rows", 0, 0)
    tri_owner = owner[jnp.array(TRI_PIVOT, jnp.int32)]
    part = jnp.concatenate(
        [
            lax.dynamic_slice(pieces, (owner[rank // 2], 0, 0), (1, HALF, BLOCK))[0],
            lax.dynamic_slice(pieces, (tri_owner[2 * rank], HALF, 0), (1, SLICE, BLOCK))[0],
            lax.dynamic_slice(pieces, (tri_owner[2 * rank + 1], HALF + SLICE, 0), (1, SLICE, BLOCK))[0],
        ]
    )
    gathered = lax.all_gather(part, "rows", axis=0, tiled=False)
    slices = gathered[:, HALF:].reshape(TRI, SLICE, BLOCK)
    core = rank % 2
    half = lax.dynamic_slice(slices, (core * 2 * PART, 0, 0), (2 * PART, SLICE, BLOCK))
    first, second = half[:PART], half[PART:]
    first = [first] + [lax.ppermute(first, "samp", shift_y(d)) for d in MOVES]
    second = [second] + [lax.ppermute(second, "samp", shift_x(d)) for d in MOVES]
    first, second = jnp.stack(first), jnp.stack(second)
    parts = [first] + [lax.ppermute(first, "samp", shift_x(d)) for d in MOVES]
    parts += [second] + [lax.ppermute(second, "samp", shift_y(d)) for d in MOVES]
    mine = jnp.stack(parts).reshape(2, SIDE, SIDE, PART, SLICE, BLOCK)
    other = lax.ppermute(mine, "rows", [(i, i ^ 1) for i in range(RANKS)])
    here = lax.axis_index("samp")
    moves = jnp.array((0,) + MOVES, jnp.int32)
    y, x = (here // SIDE - moves + SIDE) % SIDE, (here % SIDE - moves + SIDE) % SIDE
    spots = jnp.stack([SIDE * y[None, :] + x[:, None], SIDE * y[:, None] + x[None, :]]).reshape(2, RANKS)
    solved, pairs = solve(core.reshape(1), spots, gathered, mine, other, diag_inverse)
    return solved, update(picks, right_sides, everything, pairs)


def solution(mesh):
    placed = (P("rows", None, "samp"), P("rows", None, "samp", None), P("rows", None), P(), P())
    return jax.shard_map(
        local,
        mesh=mesh,
        in_specs=placed,
        out_specs=(P(None, None, "samp"), P("rows", None, "samp")),
        check_vma=False,
    )
```

```python
import jax
import jax.numpy as jnp
from jax import lax
from jax.experimental import pallas as pl
from jax.experimental.pallas import tpu as pltpu
from jax.sharding import PartitionSpec as P

BLOCK = 128
STEPS = 8
SLOTS = 6
RANKS = 16
SLICE = BLOCK // RANKS
HALF = BLOCK // 2
TRI = 32
ROWS_PER_STEP = 18
SIDE = 4
MOVES = (1, -1, 2)
PART = 7


def shift_y(d):
    return [(i, (i // SIDE + d) % SIDE * SIDE + i % SIDE) for i in range(RANKS)]


def shift_x(d):
    return [(i, i // SIDE * SIDE + (i % SIDE + d) % SIDE) for i in range(RANKS)]


def tri(k, i):
    return k * (k - 1) // 2 + i


TRI_PIVOT = [k for k in range(STEPS) for _ in range(k)] + [STEPS - 1] * (TRI - tri(STEPS, 0))


def split(x):
    hi = x.astype(jnp.bfloat16)
    lo = (x - hi.astype(jnp.float32)).astype(jnp.bfloat16)
    return hi, lo


def dot(a, b):
    return lax.dot_general(a, b, (((1,), (0,)), ((), ())), preferred_element_type=jnp.float32)


def dot3(a, b2):
    ah, al = split(a)
    full = dot(ah, b2)
    return full[:, :BLOCK] + full[:, BLOCK:] + dot(al, b2[:, :BLOCK])


def pair(x):
    return jnp.concatenate(split(x), axis=1)


def pack_kernel(pivots, columns, sides, factor, out, rows_buf, sem_f, sem_r):
    row_count = sides.shape[0]
    place = [lax.rem(pivots[j], row_count) for j in range(STEPS)]
    factor_copies, side_copies = [], []
    for j in range(STEPS):
        copy = pltpu.make_async_copy(factor.at[place[j]], rows_buf.at[j], sem_f.at[j])
        copy.start()
        factor_copies.append(copy)
    for j in range(STEPS):
        for h in range(2):
            copy = pltpu.make_async_copy(
                sides.at[place[j], pl.ds(h * HALF, HALF)], out.at[2 * j + h, pl.ds(0, HALF)], sem_r.at[2 * j + h]
            )
            copy.start()
            side_copies.append(copy)
    for copy in factor_copies:
        copy.wait()
    for j in range(STEPS):
        at = place[j]
        for i in range(j):
            piece = jnp.zeros((SLICE, BLOCK), jnp.float32)
            for s in range(SLOTS):
                piece = jnp.where(columns[s, at] == i, rows_buf[j, s], piece)
            b = tri(j, i)
            out[b // 2, pl.ds(HALF + (b % 2) * SLICE, SLICE)] = piece
    for b in range(tri(STEPS, 0), TRI):
        out[b // 2, pl.ds(HALF + (b % 2) * SLICE, SLICE)] = jnp.zeros((SLICE, BLOCK), jnp.float32)
    for copy in side_copies:
        copy.wait()


def pack(pivots, columns, sides, factor):
    smem = pl.BlockSpec(memory_space=pltpu.SMEM)
    hbm = pl.BlockSpec(memory_space=pl.ANY)
    return pl.pallas_call(
        pack_kernel,
        out_shape=jax.ShapeDtypeStruct((RANKS, HALF + 2 * SLICE, BLOCK), jnp.float32),
        in_specs=[smem, smem, hbm, hbm],
        out_specs=pl.BlockSpec(memory_space=pltpu.VMEM),
        scratch_shapes=[
            pltpu.VMEM((STEPS, SLOTS, SLICE, BLOCK), jnp.float32),
            pltpu.SemaphoreType.DMA((STEPS,)),
            pltpu.SemaphoreType.DMA((2 * STEPS,)),
        ],
        name="pack",
    )(pivots, columns, sides, factor)


def solve_kernel(core, spots, gathered, mine, other, inverse, solved, pairs, side, blocks):
    flag = core[0]
    for pieces, base in ((mine, 2 * PART * flag), (other, 2 * PART * (1 - flag))):
        for p in range(2):
            for e in range(SIDE):
                for d in range(SIDE):
                    at = pl.multiple_of(SLICE * spots[p, SIDE * e + d], SLICE)
                    for i in range(PART):
                        blocks[base + PART * p + i, pl.ds(at, SLICE)] = pieces[p, e, d, i]

    def factor(k, i):
        return blocks[tri(k, i)]

    for j in range(STEPS):
        side[j] = gathered[2 * j : 2 * j + 2, :HALF].reshape(BLOCK, BLOCK)
    for j in range(STEPS):
        x = dot3(inverse[j], pair(side[j]))
        solved[j] = x
        x2 = pair(x)
        pairs[j] = x2
        for k in range(j + 1, STEPS):
            side[k] = side[k] - dot3(factor(k, j), x2)
    pairs[STEPS] = jnp.zeros((BLOCK, 2 * BLOCK), jnp.bfloat16)


def solve(core, spots, gathered, mine, other, inverse):
    vmem = pl.BlockSpec(memory_space=pltpu.VMEM)
    return pl.pallas_call(
        solve_kernel,
        out_shape=(
            jax.ShapeDtypeStruct((STEPS, BLOCK, BLOCK), jnp.float32),
            jax.ShapeDtypeStruct((STEPS + 1, BLOCK, 2 * BLOCK), jnp.bfloat16),
        ),
        in_specs=[pl.BlockSpec(memory_space=pltpu.SMEM)] * 2 + [vmem] * 4,
        out_specs=(vmem, vmem),
        scratch_shapes=[
            pltpu.VMEM((STEPS, BLOCK, BLOCK), jnp.float32),
            pltpu.VMEM((TRI, BLOCK, BLOCK), jnp.float32),
        ],
        name="solve",
    )(core, spots, gathered, mine, other, inverse)


def update_kernel(picks, sides, factor, pairs, out):
    step = pl.program_id(0)
    for r in range(ROWS_PER_STEP):
        row = step * ROWS_PER_STEP + r
        hi, lo, x2 = [], [], []
        for s in range(SLOTS):
            fh, fl = split(factor[:, r, s].reshape(BLOCK, BLOCK))
            hi.append(fh)
            lo.append(fl)
            x2.append(pairs[picks[row, s]])
        hi = jnp.concatenate(hi, axis=1)
        lo = jnp.concatenate(lo, axis=1)
        x2 = jnp.concatenate(x2, axis=0)
        full = dot(hi, x2)
        out[r] = sides[r] - (full[:, :BLOCK] + full[:, BLOCK:] + dot(lo, x2[:, :BLOCK]))


def update(picks, sides, factor, pairs):
    rows = sides.shape[0]
    return pl.pallas_call(
        update_kernel,
        grid=(rows // ROWS_PER_STEP,),
        out_shape=jax.ShapeDtypeStruct(sides.shape, jnp.float32),
        in_specs=[
            pl.BlockSpec(memory_space=pltpu.SMEM),
            pl.BlockSpec((ROWS_PER_STEP, BLOCK, BLOCK), lambda g: (g, 0, 0)),
            pl.BlockSpec((RANKS, ROWS_PER_STEP, SLOTS, SLICE, BLOCK), lambda g: (0, g, 0, 0, 0)),
            pl.BlockSpec((STEPS + 1, BLOCK, 2 * BLOCK), lambda g: (0, 0, 0)),
        ],
        out_specs=pl.BlockSpec((ROWS_PER_STEP, BLOCK, BLOCK), lambda g: (g, 0, 0)),
        compiler_params=pltpu.CompilerParams(vmem_limit_bytes=58 * 2**20),
        name="update",
    )(picks, sides, factor, pairs)


def around(block, shift):
    ahead = lax.ppermute(block, "samp", shift(1))
    behind = lax.ppermute(block, "samp", shift(-1))
    across = jnp.concatenate(
        [lax.ppermute(ahead[: SIDE // 2], "samp", shift(1)), lax.ppermute(behind[SIDE // 2 :], "samp", shift(-1))]
    )
    return [block, ahead, behind, across]


def local(right_sides, factor_blocks, block_columns, pivot_rows, diag_inverse):
    row_count = right_sides.shape[0]
    rank = lax.axis_index("rows")
    everything = lax.all_gather(factor_blocks, "samp", axis=0, tiled=False)

    owner = pivot_rows // row_count
    ids = rank * row_count + jnp.arange(row_count, dtype=jnp.int32)
    targets = jnp.arange(STEPS, dtype=jnp.int32)
    row_rank = STEPS + jnp.sum(jnp.where(ids[:, None] == pivot_rows[None, :], targets - STEPS, 0), axis=1)
    picks = jnp.where(block_columns < row_rank[:, None], block_columns, STEPS)

    payload = pack(pivot_rows, block_columns.T, right_sides, factor_blocks)
    pieces = lax.all_to_all(payload, "rows", 0, 0)
    tri_owner = owner[jnp.array(TRI_PIVOT, jnp.int32)]
    part = jnp.concatenate(
        [
            lax.dynamic_slice(pieces, (owner[rank // 2], 0, 0), (1, HALF, BLOCK))[0],
            lax.dynamic_slice(pieces, (tri_owner[2 * rank], HALF, 0), (1, SLICE, BLOCK))[0],
            lax.dynamic_slice(pieces, (tri_owner[2 * rank + 1], HALF + SLICE, 0), (1, SLICE, BLOCK))[0],
        ]
    )
    gathered = lax.all_gather(part, "rows", axis=0, tiled=False)
    slices = gathered[:, HALF:].reshape(TRI, SLICE, BLOCK)
    core = rank % 2
    half = lax.dynamic_slice(slices, (core * 2 * PART, 0, 0), (2 * PART, SLICE, BLOCK))
    first, second = half[:PART], half[PART:]
    first = [first] + [lax.ppermute(first, "samp", shift_y(d)) for d in MOVES]
    second = [second] + [lax.ppermute(second, "samp", shift_x(d)) for d in MOVES]
    first, second = jnp.stack(first), jnp.stack(second)
    parts = around(first, shift_x) + around(second, shift_y)
    mine = jnp.stack(parts).reshape(2, SIDE, SIDE, PART, SLICE, BLOCK)
    other = lax.ppermute(mine, "rows", [(i, i ^ 1) for i in range(RANKS)])
    here = lax.axis_index("samp")
    moves = jnp.array((0,) + MOVES, jnp.int32)
    y, x = (here // SIDE - moves + SIDE) % SIDE, (here % SIDE - moves + SIDE) % SIDE
    spots = jnp.stack([SIDE * y[None, :] + x[:, None], SIDE * y[:, None] + x[None, :]]).reshape(2, RANKS)
    solved, pairs = solve(core.reshape(1), spots, gathered, mine, other, diag_inverse)
    return solved, update(picks, right_sides, everything, pairs)


def solution(mesh):
    placed = (P("rows", None, "samp"), P("rows", None, "samp", None), P("rows", None), P(), P())
    return jax.shard_map(
        local,
        mesh=mesh,
        in_specs=placed,
        out_specs=(P(None, None, "samp"), P("rows", None, "samp")),
        check_vma=False,
    )
```

```python
import jax
import jax.numpy as jnp
from jax import lax
from jax.experimental import pallas as pl
from jax.experimental.pallas import tpu as pltpu
from jax.sharding import PartitionSpec as P

BLOCK = 128
STEPS = 8
SLOTS = 6
RANKS = 16
SLICE = BLOCK // RANKS
HALF = BLOCK // 2
TRI = 32
ROWS_PER_STEP = 18
SIDE = 4
MOVES = (1, -1, 2)
PART = 4


def shift_y(d):
    return [(i, (i // SIDE + d) % SIDE * SIDE + i % SIDE) for i in range(RANKS)]


def shift_x(d):
    return [(i, i // SIDE * SIDE + (i % SIDE + d) % SIDE) for i in range(RANKS)]


def tri(k, i):
    return k * (k - 1) // 2 + i


TRI_PIVOT = [k for k in range(STEPS) for _ in range(k)] + [STEPS - 1] * (TRI - tri(STEPS, 0))


def split(x):
    hi = x.astype(jnp.bfloat16)
    lo = (x - hi.astype(jnp.float32)).astype(jnp.bfloat16)
    return hi, lo


def dot(a, b):
    return lax.dot_general(a, b, (((1,), (0,)), ((), ())), preferred_element_type=jnp.float32)


def dot3(a, b2):
    ah, al = split(a)
    full = dot(ah, b2)
    return full[:, :BLOCK] + full[:, BLOCK:] + dot(al, b2[:, :BLOCK])


def pair(x):
    return jnp.concatenate(split(x), axis=1)


def pack_kernel(pivots, columns, sides, factor, out, rows_buf, sem_f, sem_r):
    row_count = sides.shape[0]
    place = [lax.rem(pivots[j], row_count) for j in range(STEPS)]
    factor_copies, side_copies = [], []
    for j in range(STEPS):
        copy = pltpu.make_async_copy(factor.at[place[j]], rows_buf.at[j], sem_f.at[j])
        copy.start()
        factor_copies.append(copy)
    for j in range(STEPS):
        for h in range(2):
            copy = pltpu.make_async_copy(
                sides.at[place[j], pl.ds(h * HALF, HALF)], out.at[2 * j + h, pl.ds(0, HALF)], sem_r.at[2 * j + h]
            )
            copy.start()
            side_copies.append(copy)
    for copy in factor_copies:
        copy.wait()
    for j in range(STEPS):
        at = place[j]
        for i in range(j):
            piece = jnp.zeros((SLICE, BLOCK), jnp.float32)
            for s in range(SLOTS):
                piece = jnp.where(columns[s, at] == i, rows_buf[j, s], piece)
            b = tri(j, i)
            out[b // 2, pl.ds(HALF + (b % 2) * SLICE, SLICE)] = piece
    for b in range(tri(STEPS, 0), TRI):
        out[b // 2, pl.ds(HALF + (b % 2) * SLICE, SLICE)] = jnp.zeros((SLICE, BLOCK), jnp.float32)
    for copy in side_copies:
        copy.wait()


def pack(pivots, columns, sides, factor):
    smem = pl.BlockSpec(memory_space=pltpu.SMEM)
    hbm = pl.BlockSpec(memory_space=pl.ANY)
    return pl.pallas_call(
        pack_kernel,
        out_shape=jax.ShapeDtypeStruct((RANKS, HALF + 2 * SLICE, BLOCK), jnp.float32),
        in_specs=[smem, smem, hbm, hbm],
        out_specs=pl.BlockSpec(memory_space=pltpu.VMEM),
        scratch_shapes=[
            pltpu.VMEM((STEPS, SLOTS, SLICE, BLOCK), jnp.float32),
            pltpu.SemaphoreType.DMA((STEPS,)),
            pltpu.SemaphoreType.DMA((2 * STEPS,)),
        ],
        name="pack",
    )(pivots, columns, sides, factor)


def solve_kernel(starts, spots, gathered, mine, above, far, inverse, solved, pairs, side, blocks):
    groups = (mine, above, far.at[0], far.at[1])
    for q, pieces in enumerate(groups):
        base = starts[q]
        for p in range(2):
            for e in range(SIDE):
                for d in range(SIDE):
                    at = pl.multiple_of(SLICE * spots[p, SIDE * e + d], SLICE)
                    for i in range(PART):
                        blocks[base + PART * p + i, pl.ds(at, SLICE)] = pieces[p, e, d, i]

    def factor(k, i):
        return blocks[tri(k, i)]

    for j in range(STEPS):
        side[j] = gathered[2 * j : 2 * j + 2, :HALF].reshape(BLOCK, BLOCK)
    for j in range(STEPS):
        x = dot3(inverse[j], pair(side[j]))
        solved[j] = x
        x2 = pair(x)
        pairs[j] = x2
        for k in range(j + 1, STEPS):
            side[k] = side[k] - dot3(factor(k, j), x2)
    pairs[STEPS] = jnp.zeros((BLOCK, 2 * BLOCK), jnp.bfloat16)


def solve(starts, spots, gathered, mine, above, far, inverse):
    vmem = pl.BlockSpec(memory_space=pltpu.VMEM)
    return pl.pallas_call(
        solve_kernel,
        out_shape=(
            jax.ShapeDtypeStruct((STEPS, BLOCK, BLOCK), jnp.float32),
            jax.ShapeDtypeStruct((STEPS + 1, BLOCK, 2 * BLOCK), jnp.bfloat16),
        ),
        in_specs=[pl.BlockSpec(memory_space=pltpu.SMEM)] * 2 + [vmem] * 5,
        out_specs=(vmem, vmem),
        scratch_shapes=[
            pltpu.VMEM((STEPS, BLOCK, BLOCK), jnp.float32),
            pltpu.VMEM((TRI, BLOCK, BLOCK), jnp.float32),
        ],
        name="solve",
    )(starts, spots, gathered, mine, above, far, inverse)


def update_kernel(picks, sides, factor, pairs, out):
    step = pl.program_id(0)
    for r in range(ROWS_PER_STEP):
        row = step * ROWS_PER_STEP + r
        hi, lo, x2 = [], [], []
        for s in range(SLOTS):
            fh, fl = split(factor[:, r, s].reshape(BLOCK, BLOCK))
            hi.append(fh)
            lo.append(fl)
            x2.append(pairs[picks[row, s]])
        hi = jnp.concatenate(hi, axis=1)
        lo = jnp.concatenate(lo, axis=1)
        x2 = jnp.concatenate(x2, axis=0)
        full = dot(hi, x2)
        out[r] = sides[r] - (full[:, :BLOCK] + full[:, BLOCK:] + dot(lo, x2[:, :BLOCK]))


def update(picks, sides, factor, pairs):
    rows = sides.shape[0]
    return pl.pallas_call(
        update_kernel,
        grid=(rows // ROWS_PER_STEP,),
        out_shape=jax.ShapeDtypeStruct(sides.shape, jnp.float32),
        in_specs=[
            pl.BlockSpec(memory_space=pltpu.SMEM),
            pl.BlockSpec((ROWS_PER_STEP, BLOCK, BLOCK), lambda g: (g, 0, 0)),
            pl.BlockSpec((RANKS, ROWS_PER_STEP, SLOTS, SLICE, BLOCK), lambda g: (0, g, 0, 0, 0)),
            pl.BlockSpec((STEPS + 1, BLOCK, 2 * BLOCK), lambda g: (0, 0, 0)),
        ],
        out_specs=pl.BlockSpec((ROWS_PER_STEP, BLOCK, BLOCK), lambda g: (g, 0, 0)),
        compiler_params=pltpu.CompilerParams(vmem_limit_bytes=58 * 2**20),
        name="update",
    )(picks, sides, factor, pairs)


def around(block, shift):
    ahead = lax.ppermute(block, "samp", shift(1))
    behind = lax.ppermute(block, "samp", shift(-1))
    across = jnp.concatenate(
        [lax.ppermute(ahead[: SIDE // 2], "samp", shift(1)), lax.ppermute(behind[SIDE // 2 :], "samp", shift(-1))]
    )
    return [block, ahead, behind, across]


def local(right_sides, factor_blocks, block_columns, pivot_rows, diag_inverse):
    row_count = right_sides.shape[0]
    rank = lax.axis_index("rows")
    everything = lax.all_gather(factor_blocks, "samp", axis=0, tiled=False)

    owner = pivot_rows // row_count
    ids = rank * row_count + jnp.arange(row_count, dtype=jnp.int32)
    targets = jnp.arange(STEPS, dtype=jnp.int32)
    row_rank = STEPS + jnp.sum(jnp.where(ids[:, None] == pivot_rows[None, :], targets - STEPS, 0), axis=1)
    picks = jnp.where(block_columns < row_rank[:, None], block_columns, STEPS)

    payload = pack(pivot_rows, block_columns.T, right_sides, factor_blocks)
    pieces = lax.all_to_all(payload, "rows", 0, 0)
    tri_owner = owner[jnp.array(TRI_PIVOT, jnp.int32)]
    part = jnp.concatenate(
        [
            lax.dynamic_slice(pieces, (owner[rank // 2], 0, 0), (1, HALF, BLOCK))[0],
            lax.dynamic_slice(pieces, (tri_owner[2 * rank], HALF, 0), (1, SLICE, BLOCK))[0],
            lax.dynamic_slice(pieces, (tri_owner[2 * rank + 1], HALF + SLICE, 0), (1, SLICE, BLOCK))[0],
        ]
    )
    gathered = lax.all_gather(part, "rows", axis=0, tiled=False)
    slices = gathered[:, HALF:].reshape(TRI, SLICE, BLOCK)
    quarter = rank % 4
    half = lax.dynamic_slice(slices, (quarter * 2 * PART, 0, 0), (2 * PART, SLICE, BLOCK))
    first, second = half[:PART], half[PART:]
    first = [first] + [lax.ppermute(first, "samp", shift_y(d)) for d in MOVES]
    second = [second] + [lax.ppermute(second, "samp", shift_x(d)) for d in MOVES]
    first, second = jnp.stack(first), jnp.stack(second)
    parts = around(first, shift_x) + around(second, shift_y)
    mine = jnp.stack(parts).reshape(2, SIDE, SIDE, PART, SLICE, BLOCK)
    above = lax.ppermute(mine, "rows", [(i, i ^ 2) for i in range(RANKS)])
    far = lax.ppermute(jnp.stack([mine, above]), "rows", [(i, i ^ 1) for i in range(RANKS)])
    starts = 2 * PART * (quarter ^ jnp.array([0, 2, 1, 3], jnp.int32))
    here = lax.axis_index("samp")
    moves = jnp.array((0,) + MOVES, jnp.int32)
    y, x = (here // SIDE - moves + SIDE) % SIDE, (here % SIDE - moves + SIDE) % SIDE
    spots = jnp.stack([SIDE * y[None, :] + x[:, None], SIDE * y[:, None] + x[None, :]]).reshape(2, RANKS)
    solved, pairs = solve(starts, spots, gathered, mine, above, far, diag_inverse)
    return solved, update(picks, right_sides, everything, pairs)


def solution(mesh):
    placed = (P("rows", None, "samp"), P("rows", None, "samp", None), P("rows", None), P(), P())
    return jax.shard_map(
        local,
        mesh=mesh,
        in_specs=placed,
        out_specs=(P(None, None, "samp"), P("rows", None, "samp")),
        check_vma=False,
    )
```

```python
import jax
import jax.numpy as jnp
from jax import lax
from jax.experimental import pallas as pl
from jax.experimental.pallas import tpu as pltpu
from jax.sharding import PartitionSpec as P

BLOCK = 128
STEPS = 8
SLOTS = 6
RANKS = 16
SLICE = BLOCK // RANKS
HALF = BLOCK // 2
TRI = 32
ROWS_PER_STEP = 18
SIDE = 4
MOVES = (1, -1, 2)
PART = 4


def shift_y(d):
    return [(i, (i // SIDE + d) % SIDE * SIDE + i % SIDE) for i in range(RANKS)]


def shift_x(d):
    return [(i, i // SIDE * SIDE + (i % SIDE + d) % SIDE) for i in range(RANKS)]


def tri(k, i):
    return k * (k - 1) // 2 + i


TRI_PIVOT = [k for k in range(STEPS) for _ in range(k)] + [STEPS - 1] * (TRI - tri(STEPS, 0))


def split(x):
    hi = x.astype(jnp.bfloat16)
    lo = (x - hi.astype(jnp.float32)).astype(jnp.bfloat16)
    return hi, lo


def dot(a, b):
    return lax.dot_general(a, b, (((1,), (0,)), ((), ())), preferred_element_type=jnp.float32)


def dot3(a, b2):
    ah, al = split(a)
    full = dot(ah, b2)
    return full[:, :BLOCK] + full[:, BLOCK:] + dot(al, b2[:, :BLOCK])


def pair(x):
    return jnp.concatenate(split(x), axis=1)


def pack_kernel(pivots, columns, sides, factor, out, rows_buf, sem_f, sem_r):
    row_count = sides.shape[0]
    place = [lax.rem(pivots[j], row_count) for j in range(STEPS)]
    factor_copies, side_copies = [], []
    for j in range(STEPS):
        copy = pltpu.make_async_copy(factor.at[place[j]], rows_buf.at[j], sem_f.at[j])
        copy.start()
        factor_copies.append(copy)
    for j in range(STEPS):
        for h in range(2):
            copy = pltpu.make_async_copy(
                sides.at[place[j], pl.ds(h * HALF, HALF)], out.at[2 * j + h, pl.ds(0, HALF)], sem_r.at[2 * j + h]
            )
            copy.start()
            side_copies.append(copy)
    for copy in factor_copies:
        copy.wait()
    for j in range(STEPS):
        at = place[j]
        for i in range(j):
            piece = jnp.zeros((SLICE, BLOCK), jnp.float32)
            for s in range(SLOTS):
                piece = jnp.where(columns[s, at] == i, rows_buf[j, s], piece)
            b = tri(j, i)
            out[b // 2, pl.ds(HALF + (b % 2) * SLICE, SLICE)] = piece
    for b in range(tri(STEPS, 0), TRI):
        out[b // 2, pl.ds(HALF + (b % 2) * SLICE, SLICE)] = jnp.zeros((SLICE, BLOCK), jnp.float32)
    for copy in side_copies:
        copy.wait()


def pack(pivots, columns, sides, factor):
    smem = pl.BlockSpec(memory_space=pltpu.SMEM)
    hbm = pl.BlockSpec(memory_space=pl.ANY)
    return pl.pallas_call(
        pack_kernel,
        out_shape=jax.ShapeDtypeStruct((RANKS, HALF + 2 * SLICE, BLOCK), jnp.float32),
        in_specs=[smem, smem, hbm, hbm],
        out_specs=pl.BlockSpec(memory_space=pltpu.VMEM),
        scratch_shapes=[
            pltpu.VMEM((STEPS, SLOTS, SLICE, BLOCK), jnp.float32),
            pltpu.SemaphoreType.DMA((STEPS,)),
            pltpu.SemaphoreType.DMA((2 * STEPS,)),
        ],
        name="pack",
    )(pivots, columns, sides, factor)


def solve_kernel(starts, spots, gathered, mine, above, far, inverse, solved, pairs, side, blocks):
    groups = (mine, above, far.at[0], far.at[1])
    for q, pieces in enumerate(groups):
        base = starts[q]
        for p in range(2):
            for e in range(SIDE):
                for d in range(SIDE):
                    at = pl.multiple_of(SLICE * spots[p, SIDE * e + d], SLICE)
                    for i in range(PART):
                        blocks[base + PART * p + i, pl.ds(at, SLICE)] = pieces[p, e, d, i]

    def factor(k, i):
        return blocks[tri(k, i)]

    for j in range(STEPS):
        side[j] = gathered[2 * j : 2 * j + 2, :HALF].reshape(BLOCK, BLOCK)
    for j in range(STEPS):
        x = dot3(inverse[j], pair(side[j]))
        solved[j] = x
        x2 = pair(x)
        pairs[j] = x2
        for k in range(j + 1, STEPS):
            side[k] = side[k] - dot3(factor(k, j), x2)
    pairs[STEPS] = jnp.zeros((BLOCK, 2 * BLOCK), jnp.bfloat16)


def solve(starts, spots, gathered, mine, above, far, inverse):
    vmem = pl.BlockSpec(memory_space=pltpu.VMEM)
    return pl.pallas_call(
        solve_kernel,
        out_shape=(
            jax.ShapeDtypeStruct((STEPS, BLOCK, BLOCK), jnp.float32),
            jax.ShapeDtypeStruct((STEPS + 1, BLOCK, 2 * BLOCK), jnp.bfloat16),
        ),
        in_specs=[pl.BlockSpec(memory_space=pltpu.SMEM)] * 2 + [vmem] * 5,
        out_specs=(vmem, vmem),
        scratch_shapes=[
            pltpu.VMEM((STEPS, BLOCK, BLOCK), jnp.float32),
            pltpu.VMEM((TRI, BLOCK, BLOCK), jnp.float32),
        ],
        name="solve",
    )(starts, spots, gathered, mine, above, far, inverse)


def update_kernel(picks, sides, factor, pairs, out):
    step = pl.program_id(0)
    for r in range(ROWS_PER_STEP):
        row = step * ROWS_PER_STEP + r
        hi, lo, x2 = [], [], []
        for s in range(SLOTS):
            fh, fl = split(factor[:, r, s].reshape(BLOCK, BLOCK))
            hi.append(fh)
            lo.append(fl)
            x2.append(pairs[picks[row, s]])
        hi = jnp.concatenate(hi, axis=1)
        lo = jnp.concatenate(lo, axis=1)
        x2 = jnp.concatenate(x2, axis=0)
        full = dot(hi, x2)
        out[r] = sides[r] - (full[:, :BLOCK] + full[:, BLOCK:] + dot(lo, x2[:, :BLOCK]))


def update(picks, sides, factor, pairs):
    rows = sides.shape[0]
    return pl.pallas_call(
        update_kernel,
        grid=(rows // ROWS_PER_STEP,),
        out_shape=jax.ShapeDtypeStruct(sides.shape, jnp.float32),
        in_specs=[
            pl.BlockSpec(memory_space=pltpu.SMEM),
            pl.BlockSpec((ROWS_PER_STEP, BLOCK, BLOCK), lambda g: (g, 0, 0)),
            pl.BlockSpec((RANKS, ROWS_PER_STEP, SLOTS, SLICE, BLOCK), lambda g: (0, g, 0, 0, 0)),
            pl.BlockSpec((STEPS + 1, BLOCK, 2 * BLOCK), lambda g: (0, 0, 0)),
        ],
        out_specs=pl.BlockSpec((ROWS_PER_STEP, BLOCK, BLOCK), lambda g: (g, 0, 0)),
        compiler_params=pltpu.CompilerParams(vmem_limit_bytes=58 * 2**20),
        name="update",
    )(picks, sides, factor, pairs)


def around(block, shift):
    ahead = lax.ppermute(block, "samp", shift(1))
    behind = lax.ppermute(block, "samp", shift(-1))
    across = jnp.concatenate(
        [lax.ppermute(ahead[: SIDE // 2], "samp", shift(1)), lax.ppermute(behind[SIDE // 2 :], "samp", shift(-1))]
    )
    return [block, ahead, behind, across]


def local(right_sides, factor_blocks, block_columns, pivot_rows, diag_inverse):
    row_count = right_sides.shape[0]
    rank = lax.axis_index("rows")
    everything = lax.all_gather(factor_blocks.reshape(-1, BLOCK), "samp", axis=0, tiled=False)
    everything = everything.reshape((RANKS,) + factor_blocks.shape)

    owner = pivot_rows // row_count
    ids = rank * row_count + jnp.arange(row_count, dtype=jnp.int32)
    targets = jnp.arange(STEPS, dtype=jnp.int32)
    row_rank = STEPS + jnp.sum(jnp.where(ids[:, None] == pivot_rows[None, :], targets - STEPS, 0), axis=1)
    picks = jnp.where(block_columns < row_rank[:, None], block_columns, STEPS)

    payload = pack(pivot_rows, block_columns.T, right_sides, factor_blocks)
    pieces = lax.all_to_all(payload, "rows", 0, 0)
    tri_owner = owner[jnp.array(TRI_PIVOT, jnp.int32)]
    part = jnp.concatenate(
        [
            lax.dynamic_slice(pieces, (owner[rank // 2], 0, 0), (1, HALF, BLOCK))[0],
            lax.dynamic_slice(pieces, (tri_owner[2 * rank], HALF, 0), (1, SLICE, BLOCK))[0],
            lax.dynamic_slice(pieces, (tri_owner[2 * rank + 1], HALF + SLICE, 0), (1, SLICE, BLOCK))[0],
        ]
    )
    gathered = lax.all_gather(part, "rows", axis=0, tiled=False)
    slices = gathered[:, HALF:].reshape(TRI, SLICE, BLOCK)
    quarter = rank % 4
    half = lax.dynamic_slice(slices, (quarter * 2 * PART, 0, 0), (2 * PART, SLICE, BLOCK))
    first, second = half[:PART], half[PART:]
    first = [first] + [lax.ppermute(first, "samp", shift_y(d)) for d in MOVES]
    second = [second] + [lax.ppermute(second, "samp", shift_x(d)) for d in MOVES]
    first, second = jnp.stack(first), jnp.stack(second)
    parts = around(first, shift_x) + around(second, shift_y)
    mine = jnp.stack(parts).reshape(2, SIDE, SIDE, PART, SLICE, BLOCK)
    above = lax.ppermute(mine, "rows", [(i, i ^ 2) for i in range(RANKS)])
    far = lax.ppermute(jnp.stack([mine, above]), "rows", [(i, i ^ 1) for i in range(RANKS)])
    starts = 2 * PART * (quarter ^ jnp.array([0, 2, 1, 3], jnp.int32))
    here = lax.axis_index("samp")
    moves = jnp.array((0,) + MOVES, jnp.int32)
    y, x = (here // SIDE - moves + SIDE) % SIDE, (here % SIDE - moves + SIDE) % SIDE
    spots = jnp.stack([SIDE * y[None, :] + x[:, None], SIDE * y[:, None] + x[None, :]]).reshape(2, RANKS)
    solved, pairs = solve(starts, spots, gathered, mine, above, far, diag_inverse)
    return solved, update(picks, right_sides, everything, pairs)


def solution(mesh):
    placed = (P("rows", None, "samp"), P("rows", None, "samp", None), P("rows", None), P(), P())
    return jax.shard_map(
        local,
        mesh=mesh,
        in_specs=placed,
        out_specs=(P(None, None, "samp"), P("rows", None, "samp")),
        check_vma=False,
    )
```

```python
import jax
import jax.numpy as jnp
from jax import lax
from jax.experimental import pallas as pl
from jax.experimental.pallas import tpu as pltpu
from jax.sharding import PartitionSpec as P

BLOCK = 128
STEPS = 8
SLOTS = 6
RANKS = 16
SLICE = BLOCK // RANKS
HALF = BLOCK // 2
TRI = 32
ROWS_PER_STEP = 18
SIDE = 4
MOVES = (1, -1, 2)
PART = 4


def shift_y(d):
    return [(i, (i // SIDE + d) % SIDE * SIDE + i % SIDE) for i in range(RANKS)]


def shift_x(d):
    return [(i, i // SIDE * SIDE + (i % SIDE + d) % SIDE) for i in range(RANKS)]


def tri(k, i):
    return k * (k - 1) // 2 + i


TRI_PIVOT = [k for k in range(STEPS) for _ in range(k)] + [STEPS - 1] * (TRI - tri(STEPS, 0))


def split(x):
    hi = x.astype(jnp.bfloat16)
    lo = (x - hi.astype(jnp.float32)).astype(jnp.bfloat16)
    return hi, lo


def dot(a, b):
    return lax.dot_general(a, b, (((1,), (0,)), ((), ())), preferred_element_type=jnp.float32)


def dot3(a, b2):
    ah, al = split(a)
    full = dot(ah, b2)
    return full[:, :BLOCK] + full[:, BLOCK:] + dot(al, b2[:, :BLOCK])


def pair(x):
    return jnp.concatenate(split(x), axis=1)


def pack_kernel(pivots, columns, sides, factor, out, rows_buf, sem_f, sem_r):
    row_count = sides.shape[0]
    place = [lax.rem(pivots[j], row_count) for j in range(STEPS)]
    factor_copies, side_copies = [], []
    for j in range(STEPS):
        copy = pltpu.make_async_copy(factor.at[place[j]], rows_buf.at[j], sem_f.at[j])
        copy.start()
        factor_copies.append(copy)
    for j in range(STEPS):
        for h in range(2):
            copy = pltpu.make_async_copy(
                sides.at[place[j], pl.ds(h * HALF, HALF)], out.at[2 * j + h, pl.ds(0, HALF)], sem_r.at[2 * j + h]
            )
            copy.start()
            side_copies.append(copy)
    for copy in factor_copies:
        copy.wait()
    for j in range(STEPS):
        at = place[j]
        for i in range(j):
            piece = jnp.zeros((SLICE, BLOCK), jnp.float32)
            for s in range(SLOTS):
                piece = jnp.where(columns[s, at] == i, rows_buf[j, s], piece)
            b = tri(j, i)
            out[b // 2, pl.ds(HALF + (b % 2) * SLICE, SLICE)] = piece
    for b in range(tri(STEPS, 0), TRI):
        out[b // 2, pl.ds(HALF + (b % 2) * SLICE, SLICE)] = jnp.zeros((SLICE, BLOCK), jnp.float32)
    for copy in side_copies:
        copy.wait()


def pack(pivots, columns, sides, factor):
    smem = pl.BlockSpec(memory_space=pltpu.SMEM)
    hbm = pl.BlockSpec(memory_space=pl.ANY)
    return pl.pallas_call(
        pack_kernel,
        out_shape=jax.ShapeDtypeStruct((RANKS, HALF + 2 * SLICE, BLOCK), jnp.float32),
        in_specs=[smem, smem, hbm, hbm],
        out_specs=pl.BlockSpec(memory_space=pltpu.VMEM),
        scratch_shapes=[
            pltpu.VMEM((STEPS, SLOTS, SLICE, BLOCK), jnp.float32),
            pltpu.SemaphoreType.DMA((STEPS,)),
            pltpu.SemaphoreType.DMA((2 * STEPS,)),
        ],
        name="pack",
    )(pivots, columns, sides, factor)


def solve_kernel(starts, spots, gathered, mine, above, far, inverse, solved, pairs, side, blocks):
    groups = (mine, above, far.at[0], far.at[1])
    for q, pieces in enumerate(groups):
        base = starts[q]
        for p in range(2):
            for e in range(SIDE):
                for d in range(SIDE):
                    at = pl.multiple_of(SLICE * spots[p, SIDE * e + d], SLICE)
                    for i in range(PART):
                        blocks[base + PART * p + i, pl.ds(at, SLICE)] = pieces[p, e, d, i]

    def factor(k, i):
        return blocks[tri(k, i)]

    for j in range(STEPS):
        side[j] = gathered[2 * j : 2 * j + 2, :HALF].reshape(BLOCK, BLOCK)
    for j in range(STEPS):
        x = dot3(inverse[j], pair(side[j]))
        solved[j] = x
        x2 = pair(x)
        pairs[j] = x2
        for k in range(j + 1, STEPS):
            side[k] = side[k] - dot3(factor(k, j), x2)
    pairs[STEPS] = jnp.zeros((BLOCK, 2 * BLOCK), jnp.bfloat16)


def solve(starts, spots, gathered, mine, above, far, inverse):
    vmem = pl.BlockSpec(memory_space=pltpu.VMEM)
    return pl.pallas_call(
        solve_kernel,
        out_shape=(
            jax.ShapeDtypeStruct((STEPS, BLOCK, BLOCK), jnp.float32),
            jax.ShapeDtypeStruct((STEPS + 1, BLOCK, 2 * BLOCK), jnp.bfloat16),
        ),
        in_specs=[pl.BlockSpec(memory_space=pltpu.SMEM)] * 2 + [vmem] * 5,
        out_specs=(vmem, vmem),
        scratch_shapes=[
            pltpu.VMEM((STEPS, BLOCK, BLOCK), jnp.float32),
            pltpu.VMEM((TRI, BLOCK, BLOCK), jnp.float32),
        ],
        name="solve",
    )(starts, spots, gathered, mine, above, far, inverse)


def update_kernel(picks, sides, factor, pairs, out):
    step = pl.program_id(0)
    for r in range(ROWS_PER_STEP):
        row = step * ROWS_PER_STEP + r
        hi, lo, x2 = [], [], []
        for s in range(SLOTS):
            fh, fl = split(factor[:, r, s].reshape(BLOCK, BLOCK))
            hi.append(fh)
            lo.append(fl)
            x2.append(pairs[picks[row, s]])
        hi = jnp.concatenate(hi, axis=1)
        lo = jnp.concatenate(lo, axis=1)
        x2 = jnp.concatenate(x2, axis=0)
        full = dot(hi, x2)
        out[r] = sides[r] - (full[:, :BLOCK] + full[:, BLOCK:] + dot(lo, x2[:, :BLOCK]))


def update(picks, sides, factor, pairs):
    rows = sides.shape[0]
    return pl.pallas_call(
        update_kernel,
        grid=(rows // ROWS_PER_STEP,),
        out_shape=jax.ShapeDtypeStruct(sides.shape, jnp.float32),
        in_specs=[
            pl.BlockSpec(memory_space=pltpu.SMEM),
            pl.BlockSpec((ROWS_PER_STEP, BLOCK, BLOCK), lambda g: (g, 0, 0)),
            pl.BlockSpec((RANKS, ROWS_PER_STEP, SLOTS, SLICE, BLOCK), lambda g: (0, g, 0, 0, 0)),
            pl.BlockSpec((STEPS + 1, BLOCK, 2 * BLOCK), lambda g: (0, 0, 0)),
        ],
        out_specs=pl.BlockSpec((ROWS_PER_STEP, BLOCK, BLOCK), lambda g: (g, 0, 0)),
        compiler_params=pltpu.CompilerParams(vmem_limit_bytes=58 * 2**20),
        name="update",
    )(picks, sides, factor, pairs)


def around(block, shift):
    ahead = lax.ppermute(block, "samp", shift(1))
    behind = lax.ppermute(block, "samp", shift(-1))
    across = jnp.concatenate(
        [lax.ppermute(ahead[: SIDE // 2], "samp", shift(1)), lax.ppermute(behind[SIDE // 2 :], "samp", shift(-1))]
    )
    return [block, ahead, behind, across]


def local(right_sides, factor_blocks, block_columns, pivot_rows, diag_inverse):
    row_count = right_sides.shape[0]
    rank = lax.axis_index("rows")
    everything = lax.all_gather(factor_blocks.reshape(-1, BLOCK), "samp", axis=0, tiled=False)
    everything = everything.reshape((RANKS,) + factor_blocks.shape)

    owner = pivot_rows // row_count
    ids = rank * row_count + jnp.arange(row_count, dtype=jnp.int32)
    targets = jnp.arange(STEPS, dtype=jnp.int32)
    row_rank = STEPS + jnp.sum(jnp.where(ids[:, None] == pivot_rows[None, :], targets - STEPS, 0), axis=1)
    picks = jnp.where(block_columns < row_rank[:, None], block_columns, STEPS)

    payload = pack(pivot_rows, block_columns.T, right_sides, factor_blocks)
    pieces = lax.all_to_all(payload, "rows", 0, 0)
    tri_owner = owner[jnp.array(TRI_PIVOT, jnp.int32)]
    part = jnp.concatenate(
        [
            lax.dynamic_slice(pieces, (owner[rank // 2], 0, 0), (1, HALF, BLOCK))[0],
            lax.dynamic_slice(pieces, (tri_owner[2 * rank], HALF, 0), (1, SLICE, BLOCK))[0],
            lax.dynamic_slice(pieces, (tri_owner[2 * rank + 1], HALF + SLICE, 0), (1, SLICE, BLOCK))[0],
        ]
    )
    gathered = lax.all_gather(part, "rows", axis=0, tiled=False)
    slices = gathered[:, HALF:].reshape(TRI, SLICE, BLOCK)
    quarter = rank % 4
    half = lax.dynamic_slice(slices, (quarter * 2 * PART, 0, 0), (2 * PART, SLICE, BLOCK))
    first, second = half[:PART], half[PART:]
    first, second = around(first, shift_y), around(second, shift_x)
    first, second = jnp.stack(first), jnp.stack(second)
    parts = around(first, shift_x) + around(second, shift_y)
    mine = jnp.stack(parts).reshape(2, SIDE, SIDE, PART, SLICE, BLOCK)
    above = lax.ppermute(mine, "rows", [(i, i ^ 2) for i in range(RANKS)])
    far = lax.ppermute(jnp.stack([mine, above]), "rows", [(i, i ^ 1) for i in range(RANKS)])
    starts = 2 * PART * (quarter ^ jnp.array([0, 2, 1, 3], jnp.int32))
    here = lax.axis_index("samp")
    moves = jnp.array((0,) + MOVES, jnp.int32)
    y, x = (here // SIDE - moves + SIDE) % SIDE, (here % SIDE - moves + SIDE) % SIDE
    spots = jnp.stack([SIDE * y[None, :] + x[:, None], SIDE * y[:, None] + x[None, :]]).reshape(2, RANKS)
    solved, pairs = solve(starts, spots, gathered, mine, above, far, diag_inverse)
    return solved, update(picks, right_sides, everything, pairs)


def solution(mesh):
    placed = (P("rows", None, "samp"), P("rows", None, "samp", None), P("rows", None), P(), P())
    return jax.shard_map(
        local,
        mesh=mesh,
        in_specs=placed,
        out_specs=(P(None, None, "samp"), P("rows", None, "samp")),
        check_vma=False,
    )
```
